32 devices in a mesh: seq: 8 (over z, x), head: 4 (over y, core).
Axes of the slice: x: 2, y: 2, z: 4, core: 2. Of those that a mesh axis runs over, the one named last changes fastest.
Arguments:
- queries: bfloat16 [2048, 64, 128], P('seq', 'head'), may hold values from -8 to 8
- key_vectors: bfloat16 [2048, 8, 128], P('seq', 'head'), may hold values from -8 to 8
- values: bfloat16 [2048, 8, 128], P('seq', 'head'), may hold values from -6 to 6
- grad_out: bfloat16 [2048, 64, 128], P('seq', 'head'), may hold values from -6 to 6
- key_blocks: int32 [16, 8], P('seq'), may hold values from -1 to 15, as said below
Outputs:
- grad_query: bfloat16 [8192, 2048], P(('head', 'seq'))
- grad_key: bfloat16 [1024, 2048], P(('head', 'seq'))
- grad_value: bfloat16 [1024, 2048], P(('head', 'seq'))
The draws below stay inside these ranges and needn't reach their ends.
Inputs may be any that keep to these rules, and one draw needn't show every extreme that they name: `key_blocks`: row b belongs to query block b, whose position is p_b. Each row holds p_b once; its other entries are distinct positions from p_b - 6 to p_b - 1, position 0, or -1 for unused; the order within a row is arbitrary.
All inputs are finite; a program needn't handle non-finite values.
Results may differ from the reference program's by a relative error of at most 0.0153.
Values may be sent and summed in bfloat16 or wider, within the bound.
A program may use at most 64 MiB of HBM per device.

```python
import math
import jax
import jax.numpy as jnp
from jax import lax

QH = 64
KVH = 8
HD = 128
BLK = 128
WINDOW = 6
QBLOCKS = 16
TOKENS = 2048
N_SEQ = 8


def drawn_pair(key):
    subkeys = jax.random.split(jax.random.fold_in(key, 11), 2)
    query_draw = jnp.clip(jax.random.normal(subkeys[0], (TOKENS, QH, HD), jnp.float32), -6.0, 6.0)
    key_draw = jnp.clip(jax.random.normal(subkeys[1], (TOKENS, KVH, HD), jnp.float32), -6.0, 6.0)
    return (query_draw, key_draw)


def draw_queries(key, part):
    return drawn_pair(key)[0].astype(jnp.bfloat16)


def draw_key_vectors(key, part):
    return drawn_pair(key)[1].astype(jnp.bfloat16)


def draw_key_blocks(key, part):
    subkeys = jax.random.split(jax.random.fold_in(key, 23), 4)
    block_ids = jnp.arange(QBLOCKS, dtype=jnp.int32)
    shard_ids = block_ids // 2
    positions = jnp.where(block_ids % 2 == 0, shard_ids, QBLOCKS - 1 - shard_ids)
    levels = 2 ** jax.random.randint(subkeys[0], (QBLOCKS, 1), 0, 4)
    chosen = jax.random.randint(subkeys[1], (QBLOCKS, WINDOW), 0, 8) < levels
    offsets = jnp.arange(1, WINDOW + 1, dtype=jnp.int32)
    earlier = positions[:, None] - offsets[None, :]
    window_part = jnp.where(chosen & (earlier >= 0), earlier, -1)
    residue = jax.random.randint(subkeys[3], (), 0, 4)
    skipped = (positions % 4 == residue) & (positions < N_SEQ)
    sink_part = jnp.where(jnp.logical_not(skipped) & (positions > WINDOW), 0, -1)
    entries = jnp.concatenate([positions[:, None], window_part, sink_part[:, None]], axis=1)
    shuffle_keys = jax.random.randint(subkeys[2], (QBLOCKS, WINDOW + 2), 0, 1 << 20) * (WINDOW + 2) + jnp.arange(WINDOW + 2)
    shuffle = jnp.argsort(shuffle_keys, axis=1)
    return jnp.take_along_axis(entries, shuffle, axis=1).astype(jnp.int32)


def steps_of(rng, dims, cuts, least, largest):
    def one(axis_at, blocks):
        draws = jax.random.uniform(jax.random.fold_in(jax.random.fold_in(rng, 6), axis_at), (blocks,), jnp.float32, least / len(cuts), largest / len(cuts))
        return jnp.repeat(jnp.exp(draws), dims[axis_at] // blocks).reshape((-1,) + (1,) * (len(dims) - axis_at - 1))

    level = one(*cuts[0])
    for cut in cuts[1:]:
        level = level * one(*cut)
    return level


def scatter_about(key, extent, scale, most, shards=(), kind=jnp.bfloat16):
    drawn = jax.random.normal(key, extent, jnp.float32) * scale
    if len(shards) > 0:
        drawn = steps_of(key, extent, shards, -0.22, 0.18) * drawn
    return jnp.clip(drawn, min=-most, max=most).astype(kind)


def setup_inputs(seed: int = 0) -> dict:
    seeds = jax.random.split(jax.random.key(seed), 6)
    queries = draw_queries(jax.random.fold_in(seeds[5], 71), 0)
    key_vectors = draw_key_vectors(jax.random.fold_in(seeds[5], 71), 0)
    values = scatter_about(seeds[2], (TOKENS, KVH, HD), 1.0, 6.0, ((0, 8), (1, 4)))
    grad_out = scatter_about(seeds[3], (TOKENS, QH, HD), 1.0, 6.0, ((0, 8), (1, 4)))
    key_blocks = draw_key_blocks(jax.random.fold_in(seeds[5], 71), 0)
    return dict(queries=queries, key_vectors=key_vectors, values=values, grad_out=grad_out, key_blocks=key_blocks)


def storage_block(position):
    return jnp.where(position < N_SEQ, 2 * position, 2 * (QBLOCKS - 1 - position) + 1).astype(jnp.int32)

def reference(queries, key_vectors, values, grad_out, key_blocks):
    group_size = QH // KVH
    softmax_scale = 1.0 / math.sqrt(HD)
    highest = lax.Precision.HIGHEST
    query_blocks = queries.reshape(QBLOCKS, BLK, KVH, group_size, HD)
    grad_blocks = grad_out.reshape(QBLOCKS, BLK, KVH, group_size, HD)
    key_store = key_vectors.reshape(QBLOCKS, BLK, KVH, HD)
    value_store = values.reshape(QBLOCKS, BLK, KVH, HD)
    block_ids = jnp.arange(QBLOCKS, dtype=jnp.int32)
    positions = jnp.where(block_ids % 2 == 0, block_ids // 2, QBLOCKS - 1 - block_ids // 2).astype(jnp.int32)
    token_index = jnp.arange(BLK)
    causal = token_index[None, :] <= token_index[:, None]

    def one_block(running, block_item):
        key_total, value_total = running
        query_block, grad_block, listed, position = block_item
        is_valid = listed >= 0
        sources = storage_block(jnp.maximum(listed, 0))
        key_side = key_store[sources].astype(jnp.float32)
        value_side = value_store[sources].astype(jnp.float32)
        query_side = query_block.astype(jnp.float32)
        grad_side = grad_block.astype(jnp.float32)
        allowed = is_valid[:, None, None] & (causal[None] | (listed != position)[:, None, None])
        allowed = jnp.transpose(allowed, (1, 0, 2))[None, None]
        scores = jnp.einsum('ihgd,lthd->hgilt', query_side, key_side, precision=highest) * softmax_scale
        row_max = lax.optimization_barrier(jnp.max(jnp.where(allowed, scores, -jnp.inf), axis=(3, 4), keepdims=True))
        row_sum = lax.optimization_barrier(jnp.sum(jnp.where(allowed, jnp.exp(scores - row_max), 0.0), axis=(3, 4), keepdims=True))
        log_norm = row_max + jnp.log(row_sum)
        attn_probs = jnp.where(allowed, jnp.exp(scores - log_norm), 0.0)
        attn_low = lax.optimization_barrier(attn_probs.astype(jnp.bfloat16)).astype(jnp.float32)
        attn_out = jnp.einsum('hgilt,lthd->ihgd', attn_low, value_side, precision=highest)
        row_delta = jnp.einsum('ihgd,ihgd->hgi', grad_side, attn_out, precision=highest)
        grad_probs = jnp.einsum('ihgd,lthd->hgilt', grad_side, value_side, precision=highest)
        grad_scores = attn_probs * (grad_probs - row_delta[:, :, :, None, None])
        scores_low = lax.optimization_barrier(grad_scores.astype(jnp.bfloat16)).astype(jnp.float32)
        grad_query = jnp.einsum('hgilt,lthd->ihgd', scores_low, key_side, precision=highest) * softmax_scale
        grad_key = jnp.einsum('hgilt,ihgd->lthd', scores_low, query_side, precision=highest) * softmax_scale
        grad_value = jnp.einsum('hgilt,ihgd->lthd', attn_low, grad_side, precision=highest)
        keep_rows = is_valid[:, None, None, None]
        key_total = key_total.at[sources].add(jnp.where(keep_rows, grad_key, 0.0))
        value_total = value_total.at[sources].add(jnp.where(keep_rows, grad_value, 0.0))
        return ((key_total, value_total), grad_query.astype(jnp.bfloat16))
    zero_grads = jnp.zeros((QBLOCKS, BLK, KVH, HD), jnp.float32)
    totals, query_parts = lax.scan(one_block, (zero_grads, zero_grads), (query_blocks, grad_blocks, key_blocks, positions))
    grad_query = query_parts.reshape(TOKENS, QH * HD).T
    grad_key = totals[0].reshape(TOKENS, KVH * HD).T.astype(jnp.bfloat16)
    grad_value = totals[1].reshape(TOKENS, KVH * HD).T.astype(jnp.bfloat16)
    return (grad_query, grad_key, grad_value)
```

```python
import functools
import math

import jax
import jax.numpy as jnp
from jax import lax
from jax.experimental import pallas as pl
from jax.experimental.pallas import tpu as pltpu
from jax.sharding import PartitionSpec as P

NN = (((1,), (0,)), ((), ()))
NT = (((1,), (1,)), ((), ()))


def dot(a, b, dims):
    return lax.dot_general(a, b, dims, preferred_element_type=jnp.float32)


def attention_kernel(
    shape,
    blocks_ref,
    places_ref,
    listed_ref,
    q_ref,
    do_ref,
    k_ref,
    v_ref,
    dq_ref,
    dkv_ref,
    kcat,
    vcat,
    kcat_t,
    bias,
    dk_acc,
    dv_acc,
    total,
):
    block_len, head_dim, group_size, slots = shape
    scale = 1.0 / math.sqrt(head_dim)
    a = pl.program_id(1)
    wide = 2 * block_len

    @pl.when(a == 0)
    def _():
        total[...] = jnp.zeros_like(total)

    for j in range(slots):
        rows = pl.ds(pl.multiple_of(blocks_ref[a, j] * block_len, block_len), block_len)
        here = pl.ds(j * block_len, block_len)
        kcat[here, :] = k_ref[rows, :]
        vcat[here, :] = v_ref[rows, :]
        kcat_t[:, here] = k_ref[rows, :].T
        off = jnp.where(listed_ref[a, j] > 0, 0.0, -jnp.inf)
        if j == 0:
            key_at = lax.broadcasted_iota(jnp.int32, (block_len, wide), 0)
            query_at = lax.broadcasted_iota(jnp.int32, (block_len, wide), 1) % block_len
            bias[here, :] = jnp.where(key_at <= query_at, 0.0, -jnp.inf)
        else:
            bias[here, :] = jnp.full((block_len, wide), off, jnp.float32)

    keys = slots * block_len

    def pair(i, carry):
        def two(ref):
            return [
                ref[:, pl.ds(pl.multiple_of((2 * i + e) * head_dim, head_dim), head_dim)]
                for e in range(2)
            ]

        q2 = jnp.concatenate(two(q_ref), axis=0)
        do2 = jnp.concatenate(two(do_ref), axis=0)
        scores = dot(kcat[...], q2, NT) * scale + bias[...]
        grad_probs = dot(vcat[...], do2, NT)
        row_max = jnp.max(scores, axis=0, keepdims=True)
        weights = jnp.exp(scores - row_max)
        probs = weights * (1.0 / jnp.sum(weights, axis=0, keepdims=True))
        low = probs.astype(jnp.bfloat16)
        delta = jnp.sum(low.astype(jnp.float32) * grad_probs, axis=0, keepdims=True)
        grad_scores = (probs * (grad_probs - delta)).astype(jnp.bfloat16)
        dq = (dot(kcat_t[...], grad_scores, NN) * scale).astype(jnp.bfloat16)
        for e in range(2):
            rows = pl.ds(pl.multiple_of((2 * i + e) * head_dim, head_dim), head_dim)
            dq_ref[rows, :] = dq[:, e * block_len : (e + 1) * block_len]
        dk = dot(grad_scores, q2, NN)
        dv = dot(low, do2, NN)

        @pl.when(i == 0)
        def _():
            dk_acc[...] = dk
            dv_acc[...] = dv

        @pl.when(i > 0)
        def _():
            dk_acc[...] += dk
            dv_acc[...] += dv

        return carry

    lax.fori_loop(0, group_size // 2, pair, 0)

    for j in range(slots):
        here = pl.ds(j * block_len, block_len)
        b = places_ref[a, j]
        total[0, b] += (dk_acc[here, :] * scale).T
        total[1, b] += dv_acc[here, :].T

    @pl.when(a == 1)
    def _():
        for b in range(total.shape[1]):
            here = pl.ds(b * block_len, block_len)
            dkv_ref[0, :, here] = total[0, b].astype(jnp.bfloat16)
            dkv_ref[1, :, here] = total[1, b].astype(jnp.bfloat16)


def per_device(queries, key_vectors, values, grad_out, key_blocks):
    n = lax.axis_size("seq")
    me = lax.axis_index("seq")
    tokens, q_heads, head_dim = queries.shape
    block_len = tokens // 2
    kv_heads = key_vectors.shape[1]
    group_size = q_heads // kv_heads
    slots = key_blocks.shape[1]
    window = slots - 2
    blocks = 2 * n

    kv = jnp.concatenate(
        [key_vectors.reshape(tokens, -1), values.reshape(tokens, -1)], axis=1
    )
    kv_all = lax.all_gather(kv, "seq", axis=0, tiled=True)

    positions = jnp.stack([me, blocks - 1 - me])
    back = jnp.concatenate(
        [jnp.zeros((1,), jnp.int32), jnp.arange(1, window + 1, dtype=jnp.int32)]
    )
    near = positions[:, None] - back[None, :]
    near_hit = jnp.any(key_blocks[:, None, :] == near[:, :, None], axis=2) & (near >= 0)
    sink_hit = jnp.any(key_blocks == 0, axis=1) & (positions > window)
    listed = jnp.concatenate([near_hit, sink_hit[:, None]], axis=1).astype(jnp.int32)
    wanted = jnp.concatenate(
        [jnp.maximum(near, 0), jnp.zeros((2, 1), jnp.int32)], axis=1
    )
    stored = jnp.where(wanted < n, 2 * wanted, 2 * (blocks - 1 - wanted) + 1).astype(jnp.int32)

    dense = blocks <= 2 * slots
    count = blocks if dense else 2 * slots
    places = stored if dense else jnp.arange(count, dtype=jnp.int32).reshape(2, slots)
    keys = slots * block_len
    width = group_size * head_dim
    shape = (block_len, head_dim, group_size, slots)
    f32, bf16 = jnp.float32, jnp.bfloat16
    dq, dkv = pl.pallas_call(
        functools.partial(attention_kernel, shape),
        grid_spec=pltpu.PrefetchScalarGridSpec(
            num_scalar_prefetch=3,
            grid=(kv_heads, 2),
            in_specs=[
                pl.BlockSpec((block_len, width), lambda g, a, *_: (a, g)),
                pl.BlockSpec((block_len, width), lambda g, a, *_: (a, g)),
                pl.BlockSpec((n * tokens, head_dim), lambda g, a, *_: (0, g)),
                pl.BlockSpec((n * tokens, head_dim), lambda g, a, *_: (0, kv_heads + g)),
            ],
            out_specs=[
                pl.BlockSpec((width, block_len), lambda g, a, *_: (g, a)),
                pl.BlockSpec((2, head_dim, count * block_len), lambda g, a, *_: (0, g, 0)),
            ],
            scratch_shapes=[
                pltpu.VMEM((keys, head_dim), bf16),
                pltpu.VMEM((keys, head_dim), bf16),
                pltpu.VMEM((head_dim, keys), bf16),
                pltpu.VMEM((keys, 2 * block_len), f32),
                pltpu.VMEM((keys, head_dim), f32),
                pltpu.VMEM((keys, head_dim), f32),
                pltpu.VMEM((2, count, head_dim, block_len), f32),
            ],
        ),
        out_shape=[
            jax.ShapeDtypeStruct((q_heads * head_dim, tokens), bf16),
            jax.ShapeDtypeStruct((2, kv_heads * head_dim, count * block_len), bf16),
        ],
        name="attention_backward",
    )(
        stored,
        places,
        listed,
        queries.reshape(tokens, -1),
        grad_out.reshape(tokens, -1),
        kv_all,
        kv_all,
    )
    dq_rows = lax.all_to_all(dq, "seq", split_axis=0, concat_axis=1, tiled=True)
    rows = kv_heads * head_dim // n
    parts = lax.all_to_all(
        dkv.reshape(2, n, rows, count * block_len), "seq", split_axis=1, concat_axis=1, tiled=True
    )
    if dense:
        dkv_rows = jnp.sum(parts.astype(f32), axis=1).astype(bf16)
    else:
        dkv_rows = placed(parts.reshape(2, n, rows, 2, slots, block_len)).astype(bf16)
    return (dq_rows, dkv_rows[0], dkv_rows[1])


def placed(parts):
    kinds, n, rows, _, slots, block_len = parts.shape
    by_position = jnp.concatenate([parts[:, :, :, 0], parts[:, ::-1, :, 1]], axis=1)
    by_position = by_position.astype(jnp.float32)
    total = by_position[:, :, :, 0]
    for back in range(1, slots - 1):
        total = total.at[:, : 2 * n - back].add(by_position[:, back:, :, back])
    total = total.at[:, 0].add(jnp.sum(by_position[:, :, :, slots - 1], axis=1))
    stored = jnp.stack([total[:, :n], total[:, n:][:, ::-1]], axis=2)
    stored = stored.reshape(kinds, 2 * n, rows, block_len)
    return jnp.transpose(stored, (0, 2, 1, 3)).reshape(kinds, rows, 2 * n * block_len)


def solution(mesh):
    return jax.shard_map(
        per_device,
        mesh=mesh,
        in_specs=(
            P("seq", "head", None),
            P("seq", "head", None),
            P("seq", "head", None),
            P("seq", "head", None),
            P("seq", None),
        ),
        out_specs=(P(("head", "seq"), None), P(("head", "seq"), None), P(("head", "seq"), None)),
        check_vma=False,
    )
```

```python
import functools
import math

import jax
import jax.numpy as jnp
from jax import lax
from jax.experimental import pallas as pl
from jax.experimental.pallas import tpu as pltpu
from jax.sharding import PartitionSpec as P

NN = (((1,), (0,)), ((), ()))
NT = (((1,), (1,)), ((), ()))


def dot(a, b, dims):
    return lax.dot_general(a, b, dims, preferred_element_type=jnp.float32)


def attention_kernel(
    shape,
    blocks_ref,
    places_ref,
    listed_ref,
    q_ref,
    do_ref,
    k_ref,
    v_ref,
    dq_ref,
    dkv_ref,
    kcat,
    vcat,
    kcat_t,
    bias,
    dk_acc,
    dv_acc,
    total,
):
    block_len, head_dim, group_size, slots = shape
    scale = 1.0 / math.sqrt(head_dim)
    a = pl.program_id(1)
    wide = 2 * block_len

    @pl.when(a == 0)
    def _():
        total[...] = jnp.zeros_like(total)

    for j in range(slots):
        rows = pl.ds(pl.multiple_of(blocks_ref[a, j] * block_len, block_len), block_len)
        here = pl.ds(j * block_len, block_len)
        kcat[here, :] = k_ref[rows, :]
        vcat[here, :] = v_ref[rows, :]
        kcat_t[:, here] = k_ref[rows, :].T
        off = jnp.where(listed_ref[a, j] > 0, 0.0, -jnp.inf)
        if j == 0:
            key_at = lax.broadcasted_iota(jnp.int32, (block_len, wide), 0)
            query_at = lax.broadcasted_iota(jnp.int32, (block_len, wide), 1) % block_len
            bias[here, :] = jnp.where(key_at <= query_at, 0.0, -jnp.inf)
        else:
            bias[here, :] = jnp.full((block_len, wide), off, jnp.float32)

    keys = slots * block_len

    def pair(i, carry):
        def two(ref):
            return [
                ref[:, pl.ds(pl.multiple_of((2 * i + e) * head_dim, head_dim), head_dim)]
                for e in range(2)
            ]

        q2 = jnp.concatenate(two(q_ref), axis=0)
        do2 = jnp.concatenate(two(do_ref), axis=0)
        scores = dot(kcat[...], q2, NT) * scale + bias[...]
        grad_probs = dot(vcat[...], do2, NT)
        row_max = jnp.max(scores, axis=0, keepdims=True)
        weights = jnp.exp(scores - row_max)
        probs = weights * (1.0 / jnp.sum(weights, axis=0, keepdims=True))
        low = probs.astype(jnp.bfloat16)
        delta = jnp.sum(low.astype(jnp.float32) * grad_probs, axis=0, keepdims=True)
        grad_scores = (probs * (grad_probs - delta)).astype(jnp.bfloat16)
        dq = (dot(kcat_t[...], grad_scores, NN) * scale).astype(jnp.bfloat16)
        for e in range(2):
            rows = pl.ds(pl.multiple_of((2 * i + e) * head_dim, head_dim), head_dim)
            dq_ref[rows, :] = dq[:, e * block_len : (e + 1) * block_len]
        dk = dot(grad_scores, q2, NN)
        dv = dot(low, do2, NN)

        @pl.when(i == 0)
        def _():
            dk_acc[...] = dk
            dv_acc[...] = dv

        @pl.when(i > 0)
        def _():
            dk_acc[...] += dk
            dv_acc[...] += dv

        return carry

    lax.fori_loop(0, group_size // 2, pair, 0)

    for j in range(slots):
        here = pl.ds(j * block_len, block_len)
        b = places_ref[a, j]
        total[0, b] += (dk_acc[here, :] * scale).T
        total[1, b] += dv_acc[here, :].T

    @pl.when(a == 1)
    def _():
        for b in range(total.shape[1]):
            here = pl.ds(b * block_len, block_len)
            dkv_ref[0, :, here] = total[0, b].astype(jnp.bfloat16)
            dkv_ref[1, :, here] = total[1, b].astype(jnp.bfloat16)


def fused_kernel(
    sizes,
    listed_ref,
    q_ref,
    do_ref,
    kv_ref,
    dq_out,
    dk_out,
    dv_out,
    kv_at,
    kcat,
    vcat,
    kcat_t,
    bias,
    dk_acc,
    dv_acc,
    total,
    dq_stage,
    stage,
    arrived,
    row_sum,
    kv_send,
    kv_recv,
    dq_send,
    dq_recv,
    part_send,
    part_recv,
):
    n, block_len, head_dim, kv_heads, group_size, slots = sizes
    window = slots - 2
    blocks = 2 * n
    pairs = group_size // 2
    per_kv = n // kv_heads
    rows = kv_heads * head_dim // n
    wide = 2 * block_len
    scale = 1.0 / math.sqrt(head_dim)
    bf16, f32 = jnp.bfloat16, jnp.float32
    me = lax.axis_index("seq")
    mine = (me, blocks - 1 - me)

    def used(device, position):
        top = blocks - 1 - device
        return (
            ((position <= device) & (position >= device - window))
            | ((position <= top) & (position >= top - window))
            | (position == 0)
        )

    def remote(src, dst, send, recv, device):
        return pltpu.make_async_remote_copy(
            src_ref=src,
            dst_ref=dst,
            send_sem=send,
            recv_sem=recv,
            device_id={"seq": device},
            device_id_type=pl.DeviceIdType.MESH,
        )

    barrier = pltpu.get_barrier_semaphore()
    for step in range(1, n):
        pl.semaphore_signal(
            barrier,
            inc=1,
            device_id={"seq": lax.rem(me + step, n)},
            device_id_type=pl.DeviceIdType.MESH,
        )
    pl.semaphore_wait(barrier, n - 1)

    def kv_copy(half, device):
        return remote(
            kv_ref.at[pl.ds(half * block_len, block_len), :],
            kv_at.at[mine[half]],
            kv_send.at[half, device],
            kv_recv.at[mine[half]],
            device,
        )

    far_first = sorted(range(1, n), key=lambda step: -min(step, n - step))
    for half in range(2):
        for step in far_first:
            device = lax.rem(me + step, n)

            @pl.when(used(device, mine[half]))
            def _():
                kv_copy(half, device).start()

    for half in range(2):
        kv_at[mine[half]] = kv_ref[pl.ds(half * block_len, block_len), :]

    def kv_wait(position):
        remote(
            kv_ref.at[pl.ds(0, block_len), :],
            kv_at.at[position],
            kv_send.at[0, me],
            kv_recv.at[position],
            me,
        ).wait_recv()

    def dq_copy(g, a, i):
        device = g * per_kv + i
        return device, remote(
            dq_stage.at[a, pl.ds(pl.multiple_of(device * wide, wide), wide), :],
            dq_out.at[:, pl.ds(pl.multiple_of(me * wide + a * block_len, block_len), block_len)],
            dq_send.at[a, device],
            dq_recv.at[a, me],
            device,
        )

    def dq_start(g, a, i):
        device, copy = dq_copy(g, a, i)

        @pl.when(device != me)
        def _():
            copy.start()

    def part_copy(g, e, b):
        device = g * per_kv + e
        return device, remote(
            stage.at[g, b, :, pl.ds(pl.multiple_of(e * rows, rows), rows), :],
            arrived.at[me, b],
            part_send.at[device, b],
            part_recv.at[me, b],
            device,
        )

    def wanted(a, j):
        top = jnp.where(a == 0, mine[0], mine[1])
        if j == slots - 1:
            return jnp.int32(0) * top
        return jnp.maximum(top - j, 0)

    def attend(g, a):
        columns = pl.ds(pl.multiple_of(g * head_dim, head_dim), head_dim)
        v_columns = pl.ds(pl.multiple_of((kv_heads + g) * head_dim, head_dim), head_dim)
        for j in range(slots):
            here = pl.ds(j * block_len, block_len)
            position = wanted(a, j)
            k_block = kv_at[position, :, columns]
            kcat[here, :] = k_block
            vcat[here, :] = kv_at[position, :, v_columns]
            kcat_t[:, here] = k_block.T
            if j == 0:
                key_at = lax.broadcasted_iota(jnp.int32, (block_len, wide), 0)
                query_at = lax.broadcasted_iota(jnp.int32, (block_len, wide), 1) % block_len
                bias[here, :] = jnp.where(key_at <= query_at, 0.0, -jnp.inf)
            else:
                off = jnp.where(listed_ref[a, j] > 0, 0.0, -jnp.inf)
                bias[here, :] = jnp.full((block_len, wide), off, f32)
        dk_acc[...] = jnp.zeros_like(dk_acc)
        dv_acc[...] = jnp.zeros_like(dv_acc)
        query_rows = pl.ds(pl.multiple_of(a * block_len, block_len), block_len)

        def pair(i, carry):
            @pl.when(i > 0)
            def _():
                dq_start(g, a, i - 1)

            first = g * group_size + 2 * i

            def two(ref):
                return jnp.concatenate(
                    [
                        ref[
                            query_rows,
                            pl.ds(pl.multiple_of((first + e) * head_dim, head_dim), head_dim),
                        ]
                        for e in range(2)
                    ],
                    axis=0,
                )

            q2 = two(q_ref)
            do2 = two(do_ref)
            scores = dot(kcat[...], q2, NT) * scale + bias[...]
            grad_probs = dot(vcat[...], do2, NT)
            row_max = jnp.max(scores, axis=0, keepdims=True)
            weights = jnp.exp(scores - row_max)
            probs = weights * (1.0 / jnp.sum(weights, axis=0, keepdims=True))
            low = probs.astype(bf16)
            delta = jnp.sum(low.astype(f32) * grad_probs, axis=0, keepdims=True)
            grad_scores = (probs * (grad_probs - delta)).astype(bf16)
            dq = (dot(kcat_t[...], grad_scores, NN) * scale).astype(bf16)
            for e in range(2):
                at = pl.ds(pl.multiple_of((first + e) * head_dim, head_dim), head_dim)
                dq_stage[a, at, :] = dq[:, e * block_len : (e + 1) * block_len]
            dk_acc[...] += dot(grad_scores, q2, NN)
            dv_acc[...] += dot(low, do2, NN)
            return carry

        lax.fori_loop(0, pairs, pair, 0)
        for j in range(slots):
            here = pl.ds(j * block_len, block_len)
            position = wanted(a, j)
            total[position, 0] += (dk_acc[here, :] * scale).T
            total[position, 1] += dv_acc[here, :].T
        dq_start(g, a, pairs - 1)

    def step_of(step, carry):
        phase, a = step // 2, lax.rem(step, 2)
        far = 1 - me // (n // 2)
        g = jnp.where(phase == 0, far, 1 - far)

        def arrivals(position, c):
            low_part = (
                (position <= me) & (position >= me - window) | (position == 0)
            )
            due = jnp.where(a == 0, low_part, used(me, position) & jnp.logical_not(low_part))
            other = (position != mine[0]) & (position != mine[1])

            @pl.when(due & other & (phase == 0))
            def _():
                kv_wait(position)

            return c

        lax.fori_loop(0, blocks, arrivals, 0)

        @pl.when(a == 0)
        def _():
            total[...] = jnp.zeros_like(total)

        attend(g, a)

        @pl.when(a == 1)
        def _():
            def finish(b, c):
                @pl.when(used(me, b))
                def _():
                    stage[g, b] = total[b].astype(bf16)

                return c

            lax.fori_loop(0, blocks, finish, 0)

            def send(b, c):
                for e in range(per_kv):
                    device, copy = part_copy(g, e, b)

                    @pl.when(used(me, b) & (device != me))
                    def _():
                        copy.start()

                return c

            lax.fori_loop(0, blocks, send, 0)

        return carry

    lax.fori_loop(0, 2 * kv_heads, step_of, 0)

    own_rows = pl.ds(pl.multiple_of(me * wide, wide), wide)
    for a in range(2):
        at = pl.ds(pl.multiple_of(me * wide + a * block_len, block_len), block_len)
        dq_out[:, at] = dq_stage[a, own_rows, :]

    own_g = me // per_kv
    part_rows = pl.ds(pl.multiple_of(lax.rem(me, per_kv) * rows, rows), rows)

    def own(b, c):
        row_sum[b] = jnp.zeros(row_sum.shape[1:], f32)

        @pl.when(used(me, b))
        def _():
            row_sum[b] = stage[own_g, b, :, part_rows, :].astype(f32)

        return c

    lax.fori_loop(0, blocks, own, 0)

    def gather(step, carry):
        source = lax.rem(me + step, n)

        def one(b, c):
            @pl.when(used(source, b))
            def _():
                remote(
                    stage.at[0, b, :, pl.ds(0, rows), :],
                    arrived.at[source, b],
                    part_send.at[source, b],
                    part_recv.at[source, b],
                    source,
                ).wait_recv()
                row_sum[b] += arrived[source, b].astype(f32)

            return c

        lax.fori_loop(0, blocks, one, 0)
        return carry

    lax.fori_loop(1, n, gather, 0)
    for b in range(blocks):
        at = 2 * b if b < n else 2 * (blocks - 1 - b) + 1
        here = pl.ds(at * block_len, block_len)
        dk_out[:, here] = row_sum[b, 0].astype(bf16)
        dv_out[:, here] = row_sum[b, 1].astype(bf16)

    def finish_dq(step, carry):
        other = lax.rem(me + step, n)
        for a in range(2):
            remote(
                dq_stage.at[a, pl.ds(0, wide), :],
                dq_out.at[:, pl.ds(pl.multiple_of(other * wide + a * block_len, block_len), block_len)],
                dq_send.at[a, other],
                dq_recv.at[a, other],
                other,
            ).wait_recv()
            dq_copy(0, a, other)[1].wait_send()
        for half in range(2):

            @pl.when(used(other, mine[half]))
            def _():
                kv_copy(half, other).wait_send()

        def sent(b, c):
            @pl.when(used(me, b))
            def _():
                remote(
                    stage.at[0, b, :, pl.ds(0, rows), :],
                    arrived.at[me, b],
                    part_send.at[other, b],
                    part_recv.at[me, b],
                    other,
                ).wait_send()

            return c

        lax.fori_loop(0, blocks, sent, 0)
        return carry

    lax.fori_loop(1, n, finish_dq, 0)


def fused(queries, grad_out, kv, listed, sizes):
    n, block_len, head_dim, kv_heads, group_size, slots = sizes
    blocks = 2 * n
    keys = slots * block_len
    tokens = 2 * block_len
    rows = kv_heads * head_dim // n
    f32, bf16 = jnp.float32, jnp.bfloat16
    dma = pltpu.SemaphoreType.DMA
    vmem = pl.BlockSpec(memory_space=pltpu.VMEM)
    return pl.pallas_call(
        functools.partial(fused_kernel, sizes),
        in_specs=[pl.BlockSpec(memory_space=pltpu.SMEM), vmem, vmem, vmem],
        out_specs=[vmem] * 3,
        out_shape=[
            jax.ShapeDtypeStruct((kv_heads * group_size * head_dim // n, n * tokens), bf16),
            jax.ShapeDtypeStruct((rows, n * tokens), bf16),
            jax.ShapeDtypeStruct((rows, n * tokens), bf16),
        ],
        scratch_shapes=[
            pltpu.VMEM((blocks, block_len, 2 * kv_heads * head_dim), bf16),
            pltpu.VMEM((keys, head_dim), bf16),
            pltpu.VMEM((keys, head_dim), bf16),
            pltpu.VMEM((head_dim, keys), bf16),
            pltpu.VMEM((keys, 2 * block_len), f32),
            pltpu.VMEM((keys, head_dim), f32),
            pltpu.VMEM((keys, head_dim), f32),
            pltpu.VMEM((blocks, 2, head_dim, block_len), f32),
            pltpu.VMEM((2, kv_heads * group_size * head_dim, block_len), bf16),
            pltpu.VMEM((kv_heads, blocks, 2, head_dim, block_len), bf16),
            pltpu.VMEM((n, blocks, 2, rows, block_len), bf16),
            pltpu.VMEM((blocks, 2, rows, block_len), f32),
            dma((2, n)),
            dma((blocks,)),
            dma((2, n)),
            dma((2, n)),
            dma((n, blocks)),
            dma((n, blocks)),
        ],
        compiler_params=pltpu.CompilerParams(collective_id=0, has_side_effects=True),
        name="attention_backward_exchange",
    )(listed, queries, grad_out, kv)


def per_device(queries, key_vectors, values, grad_out, key_blocks):
    n = lax.axis_size("seq")
    me = lax.axis_index("seq")
    tokens, q_heads, head_dim = queries.shape
    block_len = tokens // 2
    kv_heads = key_vectors.shape[1]
    group_size = q_heads // kv_heads
    slots = key_blocks.shape[1]
    window = slots - 2
    blocks = 2 * n

    kv = jnp.concatenate(
        [key_vectors.reshape(tokens, -1), values.reshape(tokens, -1)], axis=1
    )
    positions = jnp.stack([me, blocks - 1 - me])
    back = jnp.concatenate(
        [jnp.zeros((1,), jnp.int32), jnp.arange(1, window + 1, dtype=jnp.int32)]
    )
    near = positions[:, None] - back[None, :]
    near_hit = jnp.any(key_blocks[:, None, :] == near[:, :, None], axis=2) & (near >= 0)
    sink_hit = jnp.any(key_blocks == 0, axis=1) & (positions > window)
    listed = jnp.concatenate([near_hit, sink_hit[:, None]], axis=1).astype(jnp.int32)
    wanted = jnp.concatenate(
        [jnp.maximum(near, 0), jnp.zeros((2, 1), jnp.int32)], axis=1
    )
    stored = jnp.where(wanted < n, 2 * wanted, 2 * (blocks - 1 - wanted) + 1).astype(jnp.int32)

    dense = blocks <= 2 * slots
    count = blocks if dense else 2 * slots
    places = stored if dense else jnp.arange(count, dtype=jnp.int32).reshape(2, slots)
    if dense and kv_heads == 2 and q_heads == 2 * n and n % 2 == 0:
        sizes = (n, block_len, head_dim, kv_heads, group_size, slots)
        return tuple(
            fused(
                queries.reshape(tokens, -1), grad_out.reshape(tokens, -1), kv, listed, sizes
            )
        )
    kv_all = lax.all_gather(kv, "seq", axis=0, tiled=True)
    keys = slots * block_len
    width = group_size * head_dim
    shape = (block_len, head_dim, group_size, slots)
    f32, bf16 = jnp.float32, jnp.bfloat16
    dq, dkv = pl.pallas_call(
        functools.partial(attention_kernel, shape),
        grid_spec=pltpu.PrefetchScalarGridSpec(
            num_scalar_prefetch=3,
            grid=(kv_heads, 2),
            in_specs=[
                pl.BlockSpec((block_len, width), lambda g, a, *_: (a, g)),
                pl.BlockSpec((block_len, width), lambda g, a, *_: (a, g)),
                pl.BlockSpec((n * tokens, head_dim), lambda g, a, *_: (0, g)),
                pl.BlockSpec((n * tokens, head_dim), lambda g, a, *_: (0, kv_heads + g)),
            ],
            out_specs=[
                pl.BlockSpec((width, block_len), lambda g, a, *_: (g, a)),
                pl.BlockSpec((2, head_dim, count * block_len), lambda g, a, *_: (0, g, 0)),
            ],
            scratch_shapes=[
                pltpu.VMEM((keys, head_dim), bf16),
                pltpu.VMEM((keys, head_dim), bf16),
                pltpu.VMEM((head_dim, keys), bf16),
                pltpu.VMEM((keys, 2 * block_len), f32),
                pltpu.VMEM((keys, head_dim), f32),
                pltpu.VMEM((keys, head_dim), f32),
                pltpu.VMEM((2, count, head_dim, block_len), f32),
            ],
        ),
        out_shape=[
            jax.ShapeDtypeStruct((q_heads * head_dim, tokens), bf16),
            jax.ShapeDtypeStruct((2, kv_heads * head_dim, count * block_len), bf16),
        ],
        name="attention_backward",
    )(
        stored,
        places,
        listed,
        queries.reshape(tokens, -1),
        grad_out.reshape(tokens, -1),
        kv_all,
        kv_all,
    )
    dq_rows = lax.all_to_all(dq, "seq", split_axis=0, concat_axis=1, tiled=True)
    rows = kv_heads * head_dim // n
    parts = lax.all_to_all(
        dkv.reshape(2, n, rows, count * block_len), "seq", split_axis=1, concat_axis=1, tiled=True
    )
    if dense:
        dkv_rows = jnp.sum(parts.astype(f32), axis=1).astype(bf16)
    else:
        dkv_rows = placed(parts.reshape(2, n, rows, 2, slots, block_len)).astype(bf16)
    return (dq_rows, dkv_rows[0], dkv_rows[1])


def placed(parts):
    kinds, n, rows, _, slots, block_len = parts.shape
    by_position = jnp.concatenate([parts[:, :, :, 0], parts[:, ::-1, :, 1]], axis=1)
    by_position = by_position.astype(jnp.float32)
    total = by_position[:, :, :, 0]
    for back in range(1, slots - 1):
        total = total.at[:, : 2 * n - back].add(by_position[:, back:, :, back])
    total = total.at[:, 0].add(jnp.sum(by_position[:, :, :, slots - 1], axis=1))
    stored = jnp.stack([total[:, :n], total[:, n:][:, ::-1]], axis=2)
    stored = stored.reshape(kinds, 2 * n, rows, block_len)
    return jnp.transpose(stored, (0, 2, 1, 3)).reshape(kinds, rows, 2 * n * block_len)


def solution(mesh):
    return jax.shard_map(
        per_device,
        mesh=mesh,
        in_specs=(
            P("seq", "head", None),
            P("seq", "head", None),
            P("seq", "head", None),
            P("seq", "head", None),
            P("seq", None),
        ),
        out_specs=(P(("head", "seq"), None), P(("head", "seq"), None), P(("head", "seq"), None)),
        check_vma=False,
    )
```

```python
import functools
import math

import jax
import jax.numpy as jnp
from jax import lax
from jax.experimental import pallas as pl
from jax.experimental.pallas import tpu as pltpu
from jax.sharding import PartitionSpec as P

NN = (((1,), (0,)), ((), ()))
NT = (((1,), (1,)), ((), ()))


def dot(a, b, dims):
    return lax.dot_general(a, b, dims, preferred_element_type=jnp.float32)


def attention_kernel(
    shape,
    blocks_ref,
    places_ref,
    listed_ref,
    q_ref,
    do_ref,
    k_ref,
    v_ref,
    dq_ref,
    dkv_ref,
    kcat,
    vcat,
    kcat_t,
    bias,
    dk_acc,
    dv_acc,
    total,
):
    block_len, head_dim, group_size, slots = shape
    scale = 1.0 / math.sqrt(head_dim)
    a = pl.program_id(1)
    wide = 2 * block_len

    @pl.when(a == 0)
    def _():
        total[...] = jnp.zeros_like(total)

    for j in range(slots):
        rows = pl.ds(pl.multiple_of(blocks_ref[a, j] * block_len, block_len), block_len)
        here = pl.ds(j * block_len, block_len)
        kcat[here, :] = k_ref[rows, :]
        vcat[here, :] = v_ref[rows, :]
        kcat_t[:, here] = k_ref[rows, :].T
        off = jnp.where(listed_ref[a, j] > 0, 0.0, -jnp.inf)
        if j == 0:
            key_at = lax.broadcasted_iota(jnp.int32, (block_len, wide), 0)
            query_at = lax.broadcasted_iota(jnp.int32, (block_len, wide), 1) % block_len
            bias[here, :] = jnp.where(key_at <= query_at, 0.0, -jnp.inf)
        else:
            bias[here, :] = jnp.full((block_len, wide), off, jnp.float32)

    keys = slots * block_len

    def pair(i, carry):
        def two(ref):
            return [
                ref[:, pl.ds(pl.multiple_of((2 * i + e) * head_dim, head_dim), head_dim)]
                for e in range(2)
            ]

        q2 = jnp.concatenate(two(q_ref), axis=0)
        do2 = jnp.concatenate(two(do_ref), axis=0)
        scores = dot(kcat[...], q2, NT) * scale + bias[...]
        grad_probs = dot(vcat[...], do2, NT)
        row_max = jnp.max(scores, axis=0, keepdims=True)
        weights = jnp.exp(scores - row_max)
        probs = weights * (1.0 / jnp.sum(weights, axis=0, keepdims=True))
        low = probs.astype(jnp.bfloat16)
        delta = jnp.sum(low.astype(jnp.float32) * grad_probs, axis=0, keepdims=True)
        grad_scores = (probs * (grad_probs - delta)).astype(jnp.bfloat16)
        dq = (dot(kcat_t[...], grad_scores, NN) * scale).astype(jnp.bfloat16)
        for e in range(2):
            rows = pl.ds(pl.multiple_of((2 * i + e) * head_dim, head_dim), head_dim)
            dq_ref[rows, :] = dq[:, e * block_len : (e + 1) * block_len]
        dk = dot(grad_scores, q2, NN)
        dv = dot(low, do2, NN)

        @pl.when(i == 0)
        def _():
            dk_acc[...] = dk
            dv_acc[...] = dv

        @pl.when(i > 0)
        def _():
            dk_acc[...] += dk
            dv_acc[...] += dv

        return carry

    lax.fori_loop(0, group_size // 2, pair, 0)

    for j in range(slots):
        here = pl.ds(j * block_len, block_len)
        b = places_ref[a, j]
        total[0, b] += (dk_acc[here, :] * scale).T
        total[1, b] += dv_acc[here, :].T

    @pl.when(a == 1)
    def _():
        for b in range(total.shape[1]):
            here = pl.ds(b * block_len, block_len)
            dkv_ref[0, :, here] = total[0, b].astype(jnp.bfloat16)
            dkv_ref[1, :, here] = total[1, b].astype(jnp.bfloat16)


def fused_kernel(
    sizes,
    listed_ref,
    q_ref,
    do_ref,
    kv_ref,
    dq_out,
    dk_out,
    dv_out,
    q_heads,
    do_heads,
    kv_at,
    kcat,
    vcat,
    kcat_t,
    bias,
    dk_acc,
    dv_acc,
    total,
    dq_stage,
    stage,
    arrived,
    row_sum,
    crossing,
    kv_send,
    kv_recv,
    dq_send,
    dq_recv,
    part_send,
    part_recv,
):
    n, block_len, head_dim, kv_heads, group_size, slots = sizes
    window = slots - 2
    blocks = 2 * n
    pairs = group_size // 2
    per_kv = n // kv_heads
    rows = kv_heads * head_dim // n
    wide = 2 * block_len
    scale = 1.0 / math.sqrt(head_dim)
    bf16, f32 = jnp.bfloat16, jnp.float32
    me = lax.axis_index("seq")
    mine = (me, blocks - 1 - me)

    def used(device, position):
        top = blocks - 1 - device
        return (
            ((position <= device) & (position >= device - window))
            | ((position <= top) & (position >= top - window))
            | (position == 0)
        )

    def remote(src, dst, send, recv, device):
        return pltpu.make_async_remote_copy(
            src_ref=src,
            dst_ref=dst,
            send_sem=send,
            recv_sem=recv,
            device_id={"seq": device},
            device_id_type=pl.DeviceIdType.MESH,
        )

    barrier = pltpu.get_barrier_semaphore()
    for step in range(1, n):
        pl.semaphore_signal(
            barrier,
            inc=1,
            device_id={"seq": lax.rem(me + step, n)},
            device_id_type=pl.DeviceIdType.MESH,
        )
    pl.semaphore_wait(barrier, n - 1)

    def kv_copy(half, device):
        return remote(
            kv_ref.at[pl.ds(half * block_len, block_len), :],
            kv_at.at[mine[half]],
            kv_send.at[half, device],
            kv_recv.at[mine[half]],
            device,
        )

    far_first = sorted(range(1, n), key=lambda step: -min(step, n - step))
    for half in range(2):
        for step in far_first:
            device = lax.rem(me + step, n)

            @pl.when(used(device, mine[half]))
            def _():
                kv_copy(half, device).start()

    for half in range(2):
        kv_at[mine[half]] = kv_ref[pl.ds(half * block_len, block_len), :]

    chunk = 32

    def by_head(step, c):
        at = pl.ds(pl.multiple_of(step * chunk, chunk), chunk)
        q_heads[:, at, :] = jnp.swapaxes(q_ref[at], 0, 1)
        do_heads[:, at, :] = jnp.swapaxes(do_ref[at], 0, 1)
        return c

    lax.fori_loop(0, 2 * block_len // chunk, by_head, 0)

    def kv_wait(position):
        remote(
            kv_ref.at[pl.ds(0, block_len), :],
            kv_at.at[position],
            kv_send.at[0, me],
            kv_recv.at[position],
            me,
        ).wait_recv()

    def dq_copy(g, a, i):
        device = g * per_kv + i
        return device, remote(
            dq_stage.at[a, pl.ds(pl.multiple_of(device * wide, wide), wide), :],
            dq_out.at[:, pl.ds(pl.multiple_of(me * wide + a * block_len, block_len), block_len)],
            dq_send.at[a, device],
            dq_recv.at[a, me],
            device,
        )

    def dq_start(g, a, i):
        device, copy = dq_copy(g, a, i)

        @pl.when(device != me)
        def _():
            copy.start()

    mirror = lax.rem(me + n // 2, n)
    near = me // (n // 2)

    def used_near(half, position):
        hit = [
            jnp.where(used(half * per_kv + e, position), 1, 0) for e in range(per_kv)
        ]
        return functools.reduce(jnp.maximum, hit) > 0

    def part_copy(g, e, b):
        slot = lax.rem(me + jnp.where(g == near, 0, n // 2), n)
        return remote(
            stage.at[g, b, :, pl.ds(pl.multiple_of(e * rows, rows), rows), :],
            arrived.at[slot, b],
            part_send.at[g * per_kv + e, b],
            part_recv.at[slot, b],
            near * per_kv + e,
        )

    def cross_copy(b):
        return remote(
            crossing.at[b],
            arrived.at[me, b],
            part_send.at[mirror, b],
            part_recv.at[me, b],
            mirror,
        )

    def part_wait(slot, b):
        remote(
            crossing.at[b],
            arrived.at[slot, b],
            part_send.at[slot, b],
            part_recv.at[slot, b],
            mirror,
        ).wait_recv()

    part_rows = pl.ds(pl.multiple_of(lax.rem(me, per_kv) * rows, rows), rows)

    def add_own(g):
        def own(b, c):
            row_sum[b] = jnp.zeros(row_sum.shape[1:], f32)

            @pl.when(used(me, b))
            def _():
                row_sum[b] = stage[g, b, :, part_rows, :].astype(f32)

            return c

        lax.fori_loop(0, blocks, own, 0)

    def add_peers(shift):
        def peer(step, carry):
            source = near * per_kv + lax.rem(me + step, per_kv)
            slot = lax.rem(source + shift, n)

            def one(b, c):
                @pl.when(used(source, b))
                def _():
                    part_wait(slot, b)
                    row_sum[b] += arrived[slot, b].astype(f32)

                return c

            lax.fori_loop(0, blocks, one, 0)
            return carry

        lax.fori_loop(1, per_kv, peer, 0)

    def cross():
        add_own(1 - near)
        add_peers(n // 2)

        def pack(b, c):
            crossing[b] = row_sum[b].astype(bf16)
            return c

        lax.fori_loop(0, blocks, pack, 0)

        def go(b, c):
            @pl.when(used_near(near, b))
            def _():
                cross_copy(b).start()

            return c

        lax.fori_loop(0, blocks, go, 0)

    def wanted(a, j):
        top = jnp.where(a == 0, mine[0], mine[1])
        if j == slots - 1:
            return jnp.int32(0) * top
        return jnp.maximum(top - j, 0)

    def attend(g, a):
        columns = pl.ds(pl.multiple_of(g * head_dim, head_dim), head_dim)
        v_columns = pl.ds(pl.multiple_of((kv_heads + g) * head_dim, head_dim), head_dim)
        for j in range(slots):
            here = pl.ds(j * block_len, block_len)
            position = wanted(a, j)
            k_block = kv_at[position, :, columns]
            kcat[here, :] = k_block
            vcat[here, :] = kv_at[position, :, v_columns]
            kcat_t[:, here] = k_block.T
            if j == 0:
                key_at = lax.broadcasted_iota(jnp.int32, (block_len, wide), 0)
                query_at = lax.broadcasted_iota(jnp.int32, (block_len, wide), 1) % block_len
                bias[here, :] = jnp.where(key_at <= query_at, 0.0, -jnp.inf)
            else:
                top = jnp.where(a == 0, mine[0], mine[1])
                if j == slots - 1:
                    target, real = jnp.int32(0), top > window
                else:
                    target, real = top - j, top >= j
                hits = [jnp.where(listed_ref[a, e] == target, 1, 0) for e in range(slots)]
                hit = jnp.where(real, functools.reduce(jnp.maximum, hits), 0)
                off = jnp.where(hit > 0, 0.0, -jnp.inf)
                bias[here, :] = jnp.full((block_len, wide), off, f32)
        dk_acc[...] = jnp.zeros_like(dk_acc)
        dv_acc[...] = jnp.zeros_like(dv_acc)
        query_rows = pl.ds(pl.multiple_of(a * block_len, block_len), block_len)

        def pair(i, carry):
            @pl.when(i > 0)
            def _():
                dq_start(g, a, i - 1)

            first = g * group_size + 2 * i

            def two(ref):
                return ref[pl.ds(first, 2), query_rows, :].reshape(wide, head_dim)

            q2 = two(q_heads)
            do2 = two(do_heads)
            scores = dot(kcat[...], q2, NT) * scale + bias[...]
            grad_probs = dot(vcat[...], do2, NT)
            row_max = jnp.max(scores, axis=0, keepdims=True)
            weights = jnp.exp(scores - row_max)
            probs = weights * (1.0 / jnp.sum(weights, axis=0, keepdims=True))
            low = probs.astype(bf16)
            delta = jnp.sum(low.astype(f32) * grad_probs, axis=0, keepdims=True)
            grad_scores = (probs * (grad_probs - delta)).astype(bf16)
            dq = (dot(kcat_t[...], grad_scores, NN) * scale).astype(bf16)
            for e in range(2):
                at = pl.ds(pl.multiple_of((first + e) * head_dim, head_dim), head_dim)
                dq_stage[a, at, :] = dq[:, e * block_len : (e + 1) * block_len]
            dk_acc[...] += dot(grad_scores, q2, NN)
            dv_acc[...] += dot(low, do2, NN)
            return carry

        lax.fori_loop(0, pairs, pair, 0)
        for j in range(slots):
            here = pl.ds(j * block_len, block_len)
            position = wanted(a, j)
            total[position, 0] += (dk_acc[here, :] * scale).T
            total[position, 1] += dv_acc[here, :].T
        dq_start(g, a, pairs - 1)

    def step_of(step, carry):
        phase, a = step // 2, lax.rem(step, 2)
        g = jnp.where(phase == 0, 1 - near, near)

        def arrivals(position, c):
            low_part = (
                (position <= me) & (position >= me - window) | (position == 0)
            )
            due = jnp.where(a == 0, low_part, used(me, position) & jnp.logical_not(low_part))
            other = (position != mine[0]) & (position != mine[1])

            @pl.when(due & other & (phase == 0))
            def _():
                kv_wait(position)

            return c

        lax.fori_loop(0, blocks, arrivals, 0)

        @pl.when(a == 0)
        def _():
            total[...] = jnp.zeros_like(total)

        @pl.when(step == 2 * kv_heads - 1)
        def _():
            cross()

        attend(g, a)

        @pl.when(a == 1)
        def _():
            def finish(b, c):
                @pl.when(used(me, b))
                def _():
                    stage[g, b] = total[b].astype(bf16)

                return c

            lax.fori_loop(0, blocks, finish, 0)

            def send(b, c):
                for e in range(per_kv):
                    @pl.when(used(me, b) & (lax.rem(me, per_kv) != e))
                    def _():
                        part_copy(g, e, b).start()

                return c

            lax.fori_loop(0, blocks, send, 0)

        return carry

    lax.fori_loop(0, 2 * kv_heads, step_of, 0)

    own_rows = pl.ds(pl.multiple_of(me * wide, wide), wide)
    for a in range(2):
        at = pl.ds(pl.multiple_of(me * wide + a * block_len, block_len), block_len)
        dq_out[:, at] = dq_stage[a, own_rows, :]

    add_own(near)
    add_peers(0)

    def crossed(b, c):
        @pl.when(used_near(1 - near, b))
        def _():
            part_wait(mirror, b)
            row_sum[b] += arrived[mirror, b].astype(f32)

        return c

    lax.fori_loop(0, blocks, crossed, 0)
    for b in range(blocks):
        at = 2 * b if b < n else 2 * (blocks - 1 - b) + 1
        here = pl.ds(at * block_len, block_len)
        dk_out[:, here] = row_sum[b, 0].astype(bf16)
        dv_out[:, here] = row_sum[b, 1].astype(bf16)

    def finish_dq(step, carry):
        other = lax.rem(me + step, n)
        for a in range(2):
            remote(
                dq_stage.at[a, pl.ds(0, wide), :],
                dq_out.at[:, pl.ds(pl.multiple_of(other * wide + a * block_len, block_len), block_len)],
                dq_send.at[a, other],
                dq_recv.at[a, other],
                other,
            ).wait_recv()
            dq_copy(0, a, other)[1].wait_send()
        for half in range(2):

            @pl.when(used(other, mine[half]))
            def _():
                kv_copy(half, other).wait_send()
        return carry

    lax.fori_loop(1, n, finish_dq, 0)

    def sent(b, c):
        for e in range(per_kv):
            for g in range(kv_heads):

                @pl.when(used(me, b) & (lax.rem(me, per_kv) != e))
                def _():
                    part_copy(g, e, b).wait_send()

        @pl.when(used_near(near, b))
        def _():
            cross_copy(b).wait_send()

        return c

    lax.fori_loop(0, blocks, sent, 0)


def fused(queries, grad_out, kv, listed, sizes):
    n, block_len, head_dim, kv_heads, group_size, slots = sizes
    blocks = 2 * n
    keys = slots * block_len
    tokens = 2 * block_len
    rows = kv_heads * head_dim // n
    f32, bf16 = jnp.float32, jnp.bfloat16
    dma = pltpu.SemaphoreType.DMA
    vmem = pl.BlockSpec(memory_space=pltpu.VMEM)
    return pl.pallas_call(
        functools.partial(fused_kernel, sizes),
        in_specs=[pl.BlockSpec(memory_space=pltpu.SMEM), vmem, vmem, vmem],
        out_specs=[vmem] * 3,
        out_shape=[
            jax.ShapeDtypeStruct((kv_heads * group_size * head_dim // n, n * tokens), bf16),
            jax.ShapeDtypeStruct((rows, n * tokens), bf16),
            jax.ShapeDtypeStruct((rows, n * tokens), bf16),
        ],
        scratch_shapes=[
            pltpu.VMEM((kv_heads * group_size, tokens, head_dim), bf16),
            pltpu.VMEM((kv_heads * group_size, tokens, head_dim), bf16),
            pltpu.VMEM((blocks, block_len, 2 * kv_heads * head_dim), bf16),
            pltpu.VMEM((keys, head_dim), bf16),
            pltpu.VMEM((keys, head_dim), bf16),
            pltpu.VMEM((head_dim, keys), bf16),
            pltpu.VMEM((keys, 2 * block_len), f32),
            pltpu.VMEM((keys, head_dim), f32),
            pltpu.VMEM((keys, head_dim), f32),
            pltpu.VMEM((blocks, 2, head_dim, block_len), f32),
            pltpu.VMEM((2, kv_heads * group_size * head_dim, block_len), bf16),
            pltpu.VMEM((kv_heads, blocks, 2, head_dim, block_len), bf16),
            pltpu.VMEM((n, blocks, 2, rows, block_len), bf16),
            pltpu.VMEM((blocks, 2, rows, block_len), f32),
            pltpu.VMEM((blocks, 2, rows, block_len), bf16),
            dma((2, n)),
            dma((blocks,)),
            dma((2, n)),
            dma((2, n)),
            dma((n, blocks)),
            dma((n, blocks)),
        ],
        compiler_params=pltpu.CompilerParams(collective_id=0, has_side_effects=True),
        name="attention_backward_exchange",
    )(listed, queries, grad_out, kv)


def per_device(queries, key_vectors, values, grad_out, key_blocks):
    n = lax.axis_size("seq")
    me = lax.axis_index("seq")
    tokens, q_heads, head_dim = queries.shape
    block_len = tokens // 2
    kv_heads = key_vectors.shape[1]
    group_size = q_heads // kv_heads
    slots = key_blocks.shape[1]
    window = slots - 2
    blocks = 2 * n

    kv = jnp.concatenate(
        [key_vectors.reshape(tokens, -1), values.reshape(tokens, -1)], axis=1
    )
    positions = jnp.stack([me, blocks - 1 - me])
    back = jnp.concatenate(
        [jnp.zeros((1,), jnp.int32), jnp.arange(1, window + 1, dtype=jnp.int32)]
    )
    near = positions[:, None] - back[None, :]
    near_hit = jnp.any(key_blocks[:, None, :] == near[:, :, None], axis=2) & (near >= 0)
    sink_hit = jnp.any(key_blocks == 0, axis=1) & (positions > window)
    listed = jnp.concatenate([near_hit, sink_hit[:, None]], axis=1).astype(jnp.int32)
    wanted = jnp.concatenate(
        [jnp.maximum(near, 0), jnp.zeros((2, 1), jnp.int32)], axis=1
    )
    stored = jnp.where(wanted < n, 2 * wanted, 2 * (blocks - 1 - wanted) + 1).astype(jnp.int32)

    dense = blocks <= 2 * slots
    count = blocks if dense else 2 * slots
    places = stored if dense else jnp.arange(count, dtype=jnp.int32).reshape(2, slots)
    if dense and kv_heads == 2 and q_heads == 2 * n and n % 2 == 0:
        sizes = (n, block_len, head_dim, kv_heads, group_size, slots)
        return tuple(
            fused(queries, grad_out, kv, key_blocks, sizes)
        )
    kv_all = lax.all_gather(kv, "seq", axis=0, tiled=True)
    keys = slots * block_len
    width = group_size * head_dim
    shape = (block_len, head_dim, group_size, slots)
    f32, bf16 = jnp.float32, jnp.bfloat16
    dq, dkv = pl.pallas_call(
        functools.partial(attention_kernel, shape),
        grid_spec=pltpu.PrefetchScalarGridSpec(
            num_scalar_prefetch=3,
            grid=(kv_heads, 2),
            in_specs=[
                pl.BlockSpec((block_len, width), lambda g, a, *_: (a, g)),
                pl.BlockSpec((block_len, width), lambda g, a, *_: (a, g)),
                pl.BlockSpec((n * tokens, head_dim), lambda g, a, *_: (0, g)),
                pl.BlockSpec((n * tokens, head_dim), lambda g, a, *_: (0, kv_heads + g)),
            ],
            out_specs=[
                pl.BlockSpec((width, block_len), lambda g, a, *_: (g, a)),
                pl.BlockSpec((2, head_dim, count * block_len), lambda g, a, *_: (0, g, 0)),
            ],
            scratch_shapes=[
                pltpu.VMEM((keys, head_dim), bf16),
                pltpu.VMEM((keys, head_dim), bf16),
                pltpu.VMEM((head_dim, keys), bf16),
                pltpu.VMEM((keys, 2 * block_len), f32),
                pltpu.VMEM((keys, head_dim), f32),
                pltpu.VMEM((keys, head_dim), f32),
                pltpu.VMEM((2, count, head_dim, block_len), f32),
            ],
        ),
        out_shape=[
            jax.ShapeDtypeStruct((q_heads * head_dim, tokens), bf16),
            jax.ShapeDtypeStruct((2, kv_heads * head_dim, count * block_len), bf16),
        ],
        name="attention_backward",
    )(
        stored,
        places,
        listed,
        queries.reshape(tokens, -1),
        grad_out.reshape(tokens, -1),
        kv_all,
        kv_all,
    )
    dq_rows = lax.all_to_all(dq, "seq", split_axis=0, concat_axis=1, tiled=True)
    rows = kv_heads * head_dim // n
    parts = lax.all_to_all(
        dkv.reshape(2, n, rows, count * block_len), "seq", split_axis=1, concat_axis=1, tiled=True
    )
    if dense:
        dkv_rows = jnp.sum(parts.astype(f32), axis=1).astype(bf16)
    else:
        dkv_rows = placed(parts.reshape(2, n, rows, 2, slots, block_len)).astype(bf16)
    return (dq_rows, dkv_rows[0], dkv_rows[1])


def placed(parts):
    kinds, n, rows, _, slots, block_len = parts.shape
    by_position = jnp.concatenate([parts[:, :, :, 0], parts[:, ::-1, :, 1]], axis=1)
    by_position = by_position.astype(jnp.float32)
    total = by_position[:, :, :, 0]
    for back in range(1, slots - 1):
        total = total.at[:, : 2 * n - back].add(by_position[:, back:, :, back])
    total = total.at[:, 0].add(jnp.sum(by_position[:, :, :, slots - 1], axis=1))
    stored = jnp.stack([total[:, :n], total[:, n:][:, ::-1]], axis=2)
    stored = stored.reshape(kinds, 2 * n, rows, block_len)
    return jnp.transpose(stored, (0, 2, 1, 3)).reshape(kinds, rows, 2 * n * block_len)


def solution(mesh):
    return jax.shard_map(
        per_device,
        mesh=mesh,
        in_specs=(
            P("seq", "head", None),
            P("seq", "head", None),
            P("seq", "head", None),
            P("seq", "head", None),
            P("seq", None),
        ),
        out_specs=(P(("head", "seq"), None), P(("head", "seq"), None), P(("head", "seq"), None)),
        check_vma=False,
    )
```

```python
import functools
import math

import jax
import jax.numpy as jnp
from jax import lax
from jax.experimental import pallas as pl
from jax.experimental.pallas import tpu as pltpu
from jax.sharding import PartitionSpec as P

NN = (((1,), (0,)), ((), ()))
NT = (((1,), (1,)), ((), ()))


def dot(a, b, dims):
    return lax.dot_general(a, b, dims, preferred_element_type=jnp.float32)


def attention_kernel(
    shape,
    blocks_ref,
    places_ref,
    listed_ref,
    q_ref,
    do_ref,
    k_ref,
    v_ref,
    dq_ref,
    dkv_ref,
    kcat,
    vcat,
    kcat_t,
    bias,
    dk_acc,
    dv_acc,
    total,
):
    block_len, head_dim, group_size, slots = shape
    scale = 1.0 / math.sqrt(head_dim)
    a = pl.program_id(1)
    wide = 2 * block_len

    @pl.when(a == 0)
    def _():
        total[...] = jnp.zeros_like(total)

    for j in range(slots):
        rows = pl.ds(pl.multiple_of(blocks_ref[a, j] * block_len, block_len), block_len)
        here = pl.ds(j * block_len, block_len)
        kcat[here, :] = k_ref[rows, :]
        vcat[here, :] = v_ref[rows, :]
        kcat_t[:, here] = k_ref[rows, :].T
        off = jnp.where(listed_ref[a, j] > 0, 0.0, -jnp.inf)
        if j == 0:
            key_at = lax.broadcasted_iota(jnp.int32, (block_len, wide), 0)
            query_at = lax.broadcasted_iota(jnp.int32, (block_len, wide), 1) % block_len
            bias[here, :] = jnp.where(key_at <= query_at, 0.0, -jnp.inf)
        else:
            bias[here, :] = jnp.full((block_len, wide), off, jnp.float32)

    keys = slots * block_len

    def pair(i, carry):
        def two(ref):
            return [
                ref[:, pl.ds(pl.multiple_of((2 * i + e) * head_dim, head_dim), head_dim)]
                for e in range(2)
            ]

        q2 = jnp.concatenate(two(q_ref), axis=0)
        do2 = jnp.concatenate(two(do_ref), axis=0)
        scores = dot(kcat[...], q2, NT) * scale + bias[...]
        grad_probs = dot(vcat[...], do2, NT)
        row_max = jnp.max(scores, axis=0, keepdims=True)
        weights = jnp.exp(scores - row_max)
        probs = weights * (1.0 / jnp.sum(weights, axis=0, keepdims=True))
        low = probs.astype(jnp.bfloat16)
        delta = jnp.sum(low.astype(jnp.float32) * grad_probs, axis=0, keepdims=True)
        grad_scores = (probs * (grad_probs - delta)).astype(jnp.bfloat16)
        dq = (dot(kcat_t[...], grad_scores, NN) * scale).astype(jnp.bfloat16)
        for e in range(2):
            rows = pl.ds(pl.multiple_of((2 * i + e) * head_dim, head_dim), head_dim)
            dq_ref[rows, :] = dq[:, e * block_len : (e + 1) * block_len]
        dk = dot(grad_scores, q2, NN)
        dv = dot(low, do2, NN)

        @pl.when(i == 0)
        def _():
            dk_acc[...] = dk
            dv_acc[...] = dv

        @pl.when(i > 0)
        def _():
            dk_acc[...] += dk
            dv_acc[...] += dv

        return carry

    lax.fori_loop(0, group_size // 2, pair, 0)

    for j in range(slots):
        here = pl.ds(j * block_len, block_len)
        b = places_ref[a, j]
        total[0, b] += (dk_acc[here, :] * scale).T
        total[1, b] += dv_acc[here, :].T

    @pl.when(a == 1)
    def _():
        for b in range(total.shape[1]):
            here = pl.ds(b * block_len, block_len)
            dkv_ref[0, :, here] = total[0, b].astype(jnp.bfloat16)
            dkv_ref[1, :, here] = total[1, b].astype(jnp.bfloat16)


def fused_kernel(
    sizes,
    listed_ref,
    q_ref,
    do_ref,
    kv_ref,
    dq_out,
    dk_out,
    dv_out,
    q_heads,
    do_heads,
    kv_at,
    kcat,
    vcat,
    kcat_t,
    bias,
    dk_acc,
    dv_acc,
    total,
    dq_stage,
    stage,
    arrived,
    row_sum,
    crossing,
    kv_send,
    kv_recv,
    dq_send,
    dq_recv,
    part_send,
    part_recv,
):
    n, block_len, head_dim, kv_heads, group_size, slots = sizes
    window = slots - 2
    blocks = 2 * n
    pairs = group_size // 2
    per_kv = n // kv_heads
    rows = kv_heads * head_dim // n
    wide = 2 * block_len
    scale = 1.0 / math.sqrt(head_dim)
    bf16, f32 = jnp.bfloat16, jnp.float32
    me = lax.axis_index("seq")
    mine = (me, blocks - 1 - me)

    def used(device, position):
        top = blocks - 1 - device
        return (
            ((position <= device) & (position >= device - window))
            | ((position <= top) & (position >= top - window))
            | (position == 0)
        )

    def remote(src, dst, send, recv, device):
        return pltpu.make_async_remote_copy(
            src_ref=src,
            dst_ref=dst,
            send_sem=send,
            recv_sem=recv,
            device_id={"seq": device},
            device_id_type=pl.DeviceIdType.MESH,
        )

    barrier = pltpu.get_barrier_semaphore()
    for step in range(1, n):
        pl.semaphore_signal(
            barrier,
            inc=1,
            device_id={"seq": lax.rem(me + step, n)},
            device_id_type=pl.DeviceIdType.MESH,
        )
    pl.semaphore_wait(barrier, n - 1)

    mirror = lax.rem(me + n // 2, n)
    near = me // (n // 2)

    def used_near(half, position):
        hit = [
            jnp.where(used(half * per_kv + e, position), 1, 0) for e in range(per_kv)
        ]
        return functools.reduce(jnp.maximum, hit) > 0

    owned = (mirror, blocks - 1 - mirror)

    def kv_copy(half, device):
        return remote(
            kv_ref.at[pl.ds(half * block_len, block_len), :],
            kv_at.at[mine[half]],
            kv_send.at[half, device],
            kv_recv.at[mine[half]],
            device,
        )

    def kv_forward(half, device):
        return remote(
            kv_at.at[owned[half]],
            kv_at.at[owned[half]],
            kv_send.at[half, lax.rem(device + n // 2, n)],
            kv_recv.at[owned[half]],
            device,
        )

    def peer_of(step):
        return near * per_kv + lax.rem(me + step, per_kv)

    for half in range(2):

        @pl.when(used_near(1 - near, mine[half]))
        def _():
            kv_copy(half, mirror).start()

    for half in range(2):
        for step in range(1, per_kv):

            @pl.when(used(peer_of(step), mine[half]))
            def _():
                kv_copy(half, peer_of(step)).start()

    for half in range(2):
        kv_at[mine[half]] = kv_ref[pl.ds(half * block_len, block_len), :]

    def kv_pass():
        for half in range(2):

            @pl.when(used_near(near, owned[half]))
            def _():
                kv_wait(owned[half])
                for step in range(1, per_kv):

                    @pl.when(used(peer_of(step), owned[half]))
                    def _():
                        kv_forward(half, peer_of(step)).start()

    def kv_wait(position):
        remote(
            kv_ref.at[pl.ds(0, block_len), :],
            kv_at.at[position],
            kv_send.at[0, me],
            kv_recv.at[position],
            me,
        ).wait_recv()

    kv_pass()

    chunk = 32

    def by_head(step, c):
        at = pl.ds(pl.multiple_of(step * chunk, chunk), chunk)
        q_heads[:, at, :] = jnp.swapaxes(q_ref[at], 0, 1)
        do_heads[:, at, :] = jnp.swapaxes(do_ref[at], 0, 1)
        return c

    lax.fori_loop(0, 2 * block_len // chunk, by_head, 0)

    def dq_copy(g, a, i):
        device = g * per_kv + i
        return device, remote(
            dq_stage.at[a, pl.ds(pl.multiple_of(device * wide, wide), wide), :],
            dq_out.at[:, pl.ds(pl.multiple_of(me * wide + a * block_len, block_len), block_len)],
            dq_send.at[a, device],
            dq_recv.at[a, me],
            device,
        )

    def dq_start(g, a, i):
        device, copy = dq_copy(g, a, i)

        @pl.when(device != me)
        def _():
            copy.start()

    def part_copy(g, e, b):
        slot = lax.rem(me + jnp.where(g == near, 0, n // 2), n)
        return remote(
            stage.at[g, b, :, pl.ds(pl.multiple_of(e * rows, rows), rows), :],
            arrived.at[slot, b],
            part_send.at[g * per_kv + e, b],
            part_recv.at[slot, b],
            near * per_kv + e,
        )

    def cross_copy(b):
        return remote(
            crossing.at[b],
            arrived.at[me, b],
            part_send.at[mirror, b],
            part_recv.at[me, b],
            mirror,
        )

    def part_wait(slot, b):
        remote(
            crossing.at[b],
            arrived.at[slot, b],
            part_send.at[slot, b],
            part_recv.at[slot, b],
            mirror,
        ).wait_recv()

    part_rows = pl.ds(pl.multiple_of(lax.rem(me, per_kv) * rows, rows), rows)

    def add_own(g):
        def own(b, c):
            row_sum[b] = jnp.zeros(row_sum.shape[1:], f32)

            @pl.when(used(me, b))
            def _():
                row_sum[b] = stage[g, b, :, part_rows, :].astype(f32)

            return c

        lax.fori_loop(0, blocks, own, 0)

    def add_peers(shift):
        def peer(step, carry):
            source = near * per_kv + lax.rem(me + step, per_kv)
            slot = lax.rem(source + shift, n)

            def one(b, c):
                @pl.when(used(source, b))
                def _():
                    part_wait(slot, b)
                    row_sum[b] += arrived[slot, b].astype(f32)

                return c

            lax.fori_loop(0, blocks, one, 0)
            return carry

        lax.fori_loop(1, per_kv, peer, 0)

    def cross():
        add_own(1 - near)
        add_peers(n // 2)

        def pack(b, c):
            crossing[b] = row_sum[b].astype(bf16)
            return c

        lax.fori_loop(0, blocks, pack, 0)

        def go(b, c):
            @pl.when(used_near(near, b))
            def _():
                cross_copy(b).start()

            return c

        lax.fori_loop(0, blocks, go, 0)

    def wanted(a, j):
        top = jnp.where(a == 0, mine[0], mine[1])
        if j == slots - 1:
            return jnp.int32(0) * top
        return jnp.maximum(top - j, 0)

    def attend(g, a):
        columns = pl.ds(pl.multiple_of(g * head_dim, head_dim), head_dim)
        v_columns = pl.ds(pl.multiple_of((kv_heads + g) * head_dim, head_dim), head_dim)
        for j in range(slots):
            here = pl.ds(j * block_len, block_len)
            position = wanted(a, j)
            k_block = kv_at[position, :, columns]
            kcat[here, :] = k_block
            vcat[here, :] = kv_at[position, :, v_columns]
            kcat_t[:, here] = k_block.T
            if j == 0:
                key_at = lax.broadcasted_iota(jnp.int32, (block_len, wide), 0)
                query_at = lax.broadcasted_iota(jnp.int32, (block_len, wide), 1) % block_len
                bias[here, :] = jnp.where(key_at <= query_at, 0.0, -jnp.inf)
            else:
                top = jnp.where(a == 0, mine[0], mine[1])
                if j == slots - 1:
                    target, real = jnp.int32(0), top > window
                else:
                    target, real = top - j, top >= j
                hits = [jnp.where(listed_ref[a, e] == target, 1, 0) for e in range(slots)]
                hit = jnp.where(real, functools.reduce(jnp.maximum, hits), 0)
                off = jnp.where(hit > 0, 0.0, -jnp.inf)
                bias[here, :] = jnp.full((block_len, wide), off, f32)
        dk_acc[...] = jnp.zeros_like(dk_acc)
        dv_acc[...] = jnp.zeros_like(dv_acc)
        query_rows = pl.ds(pl.multiple_of(a * block_len, block_len), block_len)

        def pair(i, carry):
            @pl.when(i > 0)
            def _():
                dq_start(g, a, i - 1)

            first = g * group_size + 2 * i

            def two(ref):
                return ref[pl.ds(first, 2), query_rows, :].reshape(wide, head_dim)

            q2 = two(q_heads)
            do2 = two(do_heads)
            scores = dot(kcat[...], q2, NT) * scale + bias[...]
            grad_probs = dot(vcat[...], do2, NT)
            row_max = jnp.max(scores, axis=0, keepdims=True)
            weights = jnp.exp(scores - row_max)
            probs = weights * (1.0 / jnp.sum(weights, axis=0, keepdims=True))
            low = probs.astype(bf16)
            delta = jnp.sum(low.astype(f32) * grad_probs, axis=0, keepdims=True)
            grad_scores = (probs * (grad_probs - delta)).astype(bf16)
            dq = (dot(kcat_t[...], grad_scores, NN) * scale).astype(bf16)
            for e in range(2):
                at = pl.ds(pl.multiple_of((first + e) * head_dim, head_dim), head_dim)
                dq_stage[a, at, :] = dq[:, e * block_len : (e + 1) * block_len]
            dk_acc[...] += dot(grad_scores, q2, NN)
            dv_acc[...] += dot(low, do2, NN)
            return carry

        lax.fori_loop(0, pairs, pair, 0)
        for j in range(slots):
            here = pl.ds(j * block_len, block_len)
            position = wanted(a, j)
            total[position, 0] += (dk_acc[here, :] * scale).T
            total[position, 1] += dv_acc[here, :].T
        dq_start(g, a, pairs - 1)

    def step_of(step, carry):
        phase, a = step // 2, lax.rem(step, 2)
        g = jnp.where(phase == 0, 1 - near, near)

        def arrivals(position, c):
            low_part = (
                (position <= me) & (position >= me - window) | (position == 0)
            )
            due = jnp.where(a == 0, low_part, used(me, position) & jnp.logical_not(low_part))
            other = (position != mine[0]) & (position != mine[1])
            other = other & (position != owned[0]) & (position != owned[1])

            @pl.when(due & other & (phase == 0))
            def _():
                kv_wait(position)

            return c

        lax.fori_loop(0, blocks, arrivals, 0)

        @pl.when(a == 0)
        def _():
            total[...] = jnp.zeros_like(total)

        @pl.when(step == 2 * kv_heads - 1)
        def _():
            cross()

        attend(g, a)

        @pl.when(a == 1)
        def _():
            def finish(b, c):
                @pl.when(used(me, b))
                def _():
                    stage[g, b] = total[b].astype(bf16)

                return c

            lax.fori_loop(0, blocks, finish, 0)

            def send(b, c):
                for e in range(per_kv):
                    @pl.when(used(me, b) & (lax.rem(me, per_kv) != e))
                    def _():
                        part_copy(g, e, b).start()

                return c

            lax.fori_loop(0, blocks, send, 0)

        return carry

    lax.fori_loop(0, 2 * kv_heads, step_of, 0)

    own_rows = pl.ds(pl.multiple_of(me * wide, wide), wide)
    for a in range(2):
        at = pl.ds(pl.multiple_of(me * wide + a * block_len, block_len), block_len)
        dq_out[:, at] = dq_stage[a, own_rows, :]

    add_own(near)
    add_peers(0)

    def crossed(b, c):
        @pl.when(used_near(1 - near, b))
        def _():
            part_wait(mirror, b)
            row_sum[b] += arrived[mirror, b].astype(f32)

        return c

    lax.fori_loop(0, blocks, crossed, 0)
    for b in range(blocks):
        at = 2 * b if b < n else 2 * (blocks - 1 - b) + 1
        here = pl.ds(at * block_len, block_len)
        dk_out[:, here] = row_sum[b, 0].astype(bf16)
        dv_out[:, here] = row_sum[b, 1].astype(bf16)

    def finish_dq(step, carry):
        other = lax.rem(me + step, n)
        for a in range(2):
            remote(
                dq_stage.at[a, pl.ds(0, wide), :],
                dq_out.at[:, pl.ds(pl.multiple_of(other * wide + a * block_len, block_len), block_len)],
                dq_send.at[a, other],
                dq_recv.at[a, other],
                other,
            ).wait_recv()
            dq_copy(0, a, other)[1].wait_send()
        return carry

    lax.fori_loop(1, n, finish_dq, 0)

    for half in range(2):

        @pl.when(used_near(1 - near, mine[half]))
        def _():
            kv_copy(half, mirror).wait_send()

        for step in range(1, per_kv):

            @pl.when(used(peer_of(step), mine[half]))
            def _():
                kv_copy(half, peer_of(step)).wait_send()

            @pl.when(used_near(near, owned[half]) & used(peer_of(step), owned[half]))
            def _():
                kv_forward(half, peer_of(step)).wait_send()

    def sent(b, c):
        for e in range(per_kv):
            for g in range(kv_heads):

                @pl.when(used(me, b) & (lax.rem(me, per_kv) != e))
                def _():
                    part_copy(g, e, b).wait_send()

        @pl.when(used_near(near, b))
        def _():
            cross_copy(b).wait_send()

        return c

    lax.fori_loop(0, blocks, sent, 0)


def fused(queries, grad_out, kv, listed, sizes):
    n, block_len, head_dim, kv_heads, group_size, slots = sizes
    blocks = 2 * n
    keys = slots * block_len
    tokens = 2 * block_len
    rows = kv_heads * head_dim // n
    f32, bf16 = jnp.float32, jnp.bfloat16
    dma = pltpu.SemaphoreType.DMA
    vmem = pl.BlockSpec(memory_space=pltpu.VMEM)
    return pl.pallas_call(
        functools.partial(fused_kernel, sizes),
        in_specs=[pl.BlockSpec(memory_space=pltpu.SMEM), vmem, vmem, vmem],
        out_specs=[vmem] * 3,
        out_shape=[
            jax.ShapeDtypeStruct((kv_heads * group_size * head_dim // n, n * tokens), bf16),
            jax.ShapeDtypeStruct((rows, n * tokens), bf16),
            jax.ShapeDtypeStruct((rows, n * tokens), bf16),
        ],
        scratch_shapes=[
            pltpu.VMEM((kv_heads * group_size, tokens, head_dim), bf16),
            pltpu.VMEM((kv_heads * group_size, tokens, head_dim), bf16),
            pltpu.VMEM((blocks, block_len, 2 * kv_heads * head_dim), bf16),
            pltpu.VMEM((keys, head_dim), bf16),
            pltpu.VMEM((keys, head_dim), bf16),
            pltpu.VMEM((head_dim, keys), bf16),
            pltpu.VMEM((keys, 2 * block_len), f32),
            pltpu.VMEM((keys, head_dim), f32),
            pltpu.VMEM((keys, head_dim), f32),
            pltpu.VMEM((blocks, 2, head_dim, block_len), f32),
            pltpu.VMEM((2, kv_heads * group_size * head_dim, block_len), bf16),
            pltpu.VMEM((kv_heads, blocks, 2, head_dim, block_len), bf16),
            pltpu.VMEM((n, blocks, 2, rows, block_len), bf16),
            pltpu.VMEM((blocks, 2, rows, block_len), f32),
            pltpu.VMEM((blocks, 2, rows, block_len), bf16),
            dma((2, n)),
            dma((blocks,)),
            dma((2, n)),
            dma((2, n)),
            dma((n, blocks)),
            dma((n, blocks)),
        ],
        compiler_params=pltpu.CompilerParams(collective_id=0, has_side_effects=True),
        name="attention_backward_exchange",
    )(listed, queries, grad_out, kv)


def per_device(queries, key_vectors, values, grad_out, key_blocks):
    n = lax.axis_size("seq")
    me = lax.axis_index("seq")
    tokens, q_heads, head_dim = queries.shape
    block_len = tokens // 2
    kv_heads = key_vectors.shape[1]
    group_size = q_heads // kv_heads
    slots = key_blocks.shape[1]
    window = slots - 2
    blocks = 2 * n

    kv = jnp.concatenate(
        [key_vectors.reshape(tokens, -1), values.reshape(tokens, -1)], axis=1
    )
    positions = jnp.stack([me, blocks - 1 - me])
    back = jnp.concatenate(
        [jnp.zeros((1,), jnp.int32), jnp.arange(1, window + 1, dtype=jnp.int32)]
    )
    near = positions[:, None] - back[None, :]
    near_hit = jnp.any(key_blocks[:, None, :] == near[:, :, None], axis=2) & (near >= 0)
    sink_hit = jnp.any(key_blocks == 0, axis=1) & (positions > window)
    listed = jnp.concatenate([near_hit, sink_hit[:, None]], axis=1).astype(jnp.int32)
    wanted = jnp.concatenate(
        [jnp.maximum(near, 0), jnp.zeros((2, 1), jnp.int32)], axis=1
    )
    stored = jnp.where(wanted < n, 2 * wanted, 2 * (blocks - 1 - wanted) + 1).astype(jnp.int32)

    dense = blocks <= 2 * slots
    count = blocks if dense else 2 * slots
    places = stored if dense else jnp.arange(count, dtype=jnp.int32).reshape(2, slots)
    if dense and kv_heads == 2 and q_heads == 2 * n and n % 2 == 0:
        sizes = (n, block_len, head_dim, kv_heads, group_size, slots)
        return tuple(
            fused(queries, grad_out, kv, key_blocks, sizes)
        )
    kv_all = lax.all_gather(kv, "seq", axis=0, tiled=True)
    keys = slots * block_len
    width = group_size * head_dim
    shape = (block_len, head_dim, group_size, slots)
    f32, bf16 = jnp.float32, jnp.bfloat16
    dq, dkv = pl.pallas_call(
        functools.partial(attention_kernel, shape),
        grid_spec=pltpu.PrefetchScalarGridSpec(
            num_scalar_prefetch=3,
            grid=(kv_heads, 2),
            in_specs=[
                pl.BlockSpec((block_len, width), lambda g, a, *_: (a, g)),
                pl.BlockSpec((block_len, width), lambda g, a, *_: (a, g)),
                pl.BlockSpec((n * tokens, head_dim), lambda g, a, *_: (0, g)),
                pl.BlockSpec((n * tokens, head_dim), lambda g, a, *_: (0, kv_heads + g)),
            ],
            out_specs=[
                pl.BlockSpec((width, block_len), lambda g, a, *_: (g, a)),
                pl.BlockSpec((2, head_dim, count * block_len), lambda g, a, *_: (0, g, 0)),
            ],
            scratch_shapes=[
                pltpu.VMEM((keys, head_dim), bf16),
                pltpu.VMEM((keys, head_dim), bf16),
                pltpu.VMEM((head_dim, keys), bf16),
                pltpu.VMEM((keys, 2 * block_len), f32),
                pltpu.VMEM((keys, head_dim), f32),
                pltpu.VMEM((keys, head_dim), f32),
                pltpu.VMEM((2, count, head_dim, block_len), f32),
            ],
        ),
        out_shape=[
            jax.ShapeDtypeStruct((q_heads * head_dim, tokens), bf16),
            jax.ShapeDtypeStruct((2, kv_heads * head_dim, count * block_len), bf16),
        ],
        name="attention_backward",
    )(
        stored,
        places,
        listed,
        queries.reshape(tokens, -1),
        grad_out.reshape(tokens, -1),
        kv_all,
        kv_all,
    )
    dq_rows = lax.all_to_all(dq, "seq", split_axis=0, concat_axis=1, tiled=True)
    rows = kv_heads * head_dim // n
    parts = lax.all_to_all(
        dkv.reshape(2, n, rows, count * block_len), "seq", split_axis=1, concat_axis=1, tiled=True
    )
    if dense:
        dkv_rows = jnp.sum(parts.astype(f32), axis=1).astype(bf16)
    else:
        dkv_rows = placed(parts.reshape(2, n, rows, 2, slots, block_len)).astype(bf16)
    return (dq_rows, dkv_rows[0], dkv_rows[1])


def placed(parts):
    kinds, n, rows, _, slots, block_len = parts.shape
    by_position = jnp.concatenate([parts[:, :, :, 0], parts[:, ::-1, :, 1]], axis=1)
    by_position = by_position.astype(jnp.float32)
    total = by_position[:, :, :, 0]
    for back in range(1, slots - 1):
        total = total.at[:, : 2 * n - back].add(by_position[:, back:, :, back])
    total = total.at[:, 0].add(jnp.sum(by_position[:, :, :, slots - 1], axis=1))
    stored = jnp.stack([total[:, :n], total[:, n:][:, ::-1]], axis=2)
    stored = stored.reshape(kinds, 2 * n, rows, block_len)
    return jnp.transpose(stored, (0, 2, 1, 3)).reshape(kinds, rows, 2 * n * block_len)


def solution(mesh):
    return jax.shard_map(
        per_device,
        mesh=mesh,
        in_specs=(
            P("seq", "head", None),
            P("seq", "head", None),
            P("seq", "head", None),
            P("seq", "head", None),
            P("seq", None),
        ),
        out_specs=(P(("head", "seq"), None), P(("head", "seq"), None), P(("head", "seq"), None)),
        check_vma=False,
    )
```

```python
import functools
import math

import jax
import jax.numpy as jnp
from jax import lax
from jax.experimental import pallas as pl
from jax.experimental.pallas import tpu as pltpu
from jax.sharding import PartitionSpec as P

NN = (((1,), (0,)), ((), ()))
NT = (((1,), (1,)), ((), ()))


def dot(a, b, dims):
    return lax.dot_general(a, b, dims, preferred_element_type=jnp.float32)


def attention_kernel(
    shape,
    blocks_ref,
    places_ref,
    listed_ref,
    q_ref,
    do_ref,
    k_ref,
    v_ref,
    dq_ref,
    dkv_ref,
    kcat,
    vcat,
    kcat_t,
    bias,
    dk_acc,
    dv_acc,
    total,
):
    block_len, head_dim, group_size, slots = shape
    scale = 1.0 / math.sqrt(head_dim)
    a = pl.program_id(1)
    wide = 2 * block_len

    @pl.when(a == 0)
    def _():
        total[...] = jnp.zeros_like(total)

    for j in range(slots):
        rows = pl.ds(pl.multiple_of(blocks_ref[a, j] * block_len, block_len), block_len)
        here = pl.ds(j * block_len, block_len)
        kcat[here, :] = k_ref[rows, :]
        vcat[here, :] = v_ref[rows, :]
        kcat_t[:, here] = k_ref[rows, :].T
        off = jnp.where(listed_ref[a, j] > 0, 0.0, -jnp.inf)
        if j == 0:
            key_at = lax.broadcasted_iota(jnp.int32, (block_len, wide), 0)
            query_at = lax.broadcasted_iota(jnp.int32, (block_len, wide), 1) % block_len
            bias[here, :] = jnp.where(key_at <= query_at, 0.0, -jnp.inf)
        else:
            bias[here, :] = jnp.full((block_len, wide), off, jnp.float32)

    keys = slots * block_len

    def pair(i, carry):
        def two(ref):
            return [
                ref[:, pl.ds(pl.multiple_of((2 * i + e) * head_dim, head_dim), head_dim)]
                for e in range(2)
            ]

        q2 = jnp.concatenate(two(q_ref), axis=0)
        do2 = jnp.concatenate(two(do_ref), axis=0)
        scores = dot(kcat[...], q2, NT) * scale + bias[...]
        grad_probs = dot(vcat[...], do2, NT)
        row_max = jnp.max(scores, axis=0, keepdims=True)
        weights = jnp.exp(scores - row_max)
        probs = weights * (1.0 / jnp.sum(weights, axis=0, keepdims=True))
        low = probs.astype(jnp.bfloat16)
        delta = jnp.sum(low.astype(jnp.float32) * grad_probs, axis=0, keepdims=True)
        grad_scores = (probs * (grad_probs - delta)).astype(jnp.bfloat16)
        dq = (dot(kcat_t[...], grad_scores, NN) * scale).astype(jnp.bfloat16)
        for e in range(2):
            rows = pl.ds(pl.multiple_of((2 * i + e) * head_dim, head_dim), head_dim)
            dq_ref[rows, :] = dq[:, e * block_len : (e + 1) * block_len]
        dk = dot(grad_scores, q2, NN)
        dv = dot(low, do2, NN)

        @pl.when(i == 0)
        def _():
            dk_acc[...] = dk
            dv_acc[...] = dv

        @pl.when(i > 0)
        def _():
            dk_acc[...] += dk
            dv_acc[...] += dv

        return carry

    lax.fori_loop(0, group_size // 2, pair, 0)

    for j in range(slots):
        here = pl.ds(j * block_len, block_len)
        b = places_ref[a, j]
        total[0, b] += (dk_acc[here, :] * scale).T
        total[1, b] += dv_acc[here, :].T

    @pl.when(a == 1)
    def _():
        for b in range(total.shape[1]):
            here = pl.ds(b * block_len, block_len)
            dkv_ref[0, :, here] = total[0, b].astype(jnp.bfloat16)
            dkv_ref[1, :, here] = total[1, b].astype(jnp.bfloat16)


def fused_kernel(
    sizes,
    listed_ref,
    q_ref,
    do_ref,
    kv_ref,
    dq_out,
    dk_out,
    dv_out,
    q_heads,
    do_heads,
    kv_at,
    kcat,
    vcat,
    kcat_t,
    bias,
    dk_acc,
    dv_acc,
    total,
    dq_stage,
    stage,
    arrived,
    row_sum,
    crossing,
    kv_send,
    kv_recv,
    dq_send,
    dq_recv,
    part_send,
    part_recv,
):
    n, block_len, head_dim, kv_heads, group_size, slots = sizes
    window = slots - 2
    blocks = 2 * n
    pairs = group_size // 2
    per_kv = n // kv_heads
    rows = kv_heads * head_dim // n
    wide = 2 * block_len
    scale = 1.0 / math.sqrt(head_dim)
    bf16, f32 = jnp.bfloat16, jnp.float32
    me = lax.axis_index("seq")
    mine = (me, blocks - 1 - me)

    def used(device, position):
        top = blocks - 1 - device
        return (
            ((position <= device) & (position >= device - window))
            | ((position <= top) & (position >= top - window))
            | (position == 0)
        )

    def remote(src, dst, send, recv, device):
        return pltpu.make_async_remote_copy(
            src_ref=src,
            dst_ref=dst,
            send_sem=send,
            recv_sem=recv,
            device_id={"seq": device},
            device_id_type=pl.DeviceIdType.MESH,
        )

    barrier = pltpu.get_barrier_semaphore()
    for step in range(1, n):
        pl.semaphore_signal(
            barrier,
            inc=1,
            device_id={"seq": lax.rem(me + step, n)},
            device_id_type=pl.DeviceIdType.MESH,
        )
    pl.semaphore_wait(barrier, n - 1)

    mirror = lax.rem(me + n // 2, n)
    near = me // (n // 2)

    def used_near(half, position):
        hit = [
            jnp.where(used(half * per_kv + e, position), 1, 0) for e in range(per_kv)
        ]
        return functools.reduce(jnp.maximum, hit) > 0

    owned = (mirror, blocks - 1 - mirror)

    def kv_copy(half, device):
        return remote(
            kv_ref.at[pl.ds(half * block_len, block_len), :],
            kv_at.at[mine[half]],
            kv_send.at[half, device],
            kv_recv.at[mine[half]],
            device,
        )

    def kv_forward(half, device):
        return remote(
            kv_at.at[owned[half]],
            kv_at.at[owned[half]],
            kv_send.at[half, lax.rem(device + n // 2, n)],
            kv_recv.at[owned[half]],
            device,
        )

    def peer_of(step):
        return near * per_kv + lax.rem(me + step, per_kv)

    for half in range(2):

        @pl.when(used_near(1 - near, mine[half]))
        def _():
            kv_copy(half, mirror).start()

    def direct(half, now):
        for step in range(1, per_kv):

            @pl.when(used(peer_of(step), mine[half]) & now)
            def _():
                kv_copy(half, peer_of(step)).start()

    direct(0, near >= 0)
    direct(1, near == 0)

    for half in range(2):
        kv_at[mine[half]] = kv_ref[pl.ds(half * block_len, block_len), :]

    def kv_pass():
        for half in range(2):

            @pl.when(used_near(near, owned[half]))
            def _():
                kv_wait(owned[half])
                for step in range(1, per_kv):

                    @pl.when(used(peer_of(step), owned[half]))
                    def _():
                        kv_forward(half, peer_of(step)).start()

    def kv_wait(position):
        remote(
            kv_ref.at[pl.ds(0, block_len), :],
            kv_at.at[position],
            kv_send.at[0, me],
            kv_recv.at[position],
            me,
        ).wait_recv()

    chunk = 32

    def by_head(step, c):
        at = pl.ds(pl.multiple_of(step * chunk, chunk), chunk)
        q_heads[:, at, :] = jnp.swapaxes(q_ref[at], 0, 1)
        do_heads[:, at, :] = jnp.swapaxes(do_ref[at], 0, 1)
        return c

    lax.fori_loop(0, 2 * block_len // chunk, by_head, 0)

    kv_pass()
    direct(1, near == 1)

    def dq_copy(g, a, i):
        device = g * per_kv + i
        return device, remote(
            dq_stage.at[a, pl.ds(pl.multiple_of(device * wide, wide), wide), :],
            dq_out.at[:, pl.ds(pl.multiple_of(me * wide + a * block_len, block_len), block_len)],
            dq_send.at[a, device],
            dq_recv.at[a, me],
            device,
        )

    def dq_start(g, a, i):
        device, copy = dq_copy(g, a, i)

        @pl.when(device != me)
        def _():
            copy.start()

    def part_copy(g, e, b):
        slot = lax.rem(me + jnp.where(g == near, 0, n // 2), n)
        return remote(
            stage.at[g, b, :, pl.ds(pl.multiple_of(e * rows, rows), rows), :],
            arrived.at[slot, b],
            part_send.at[g * per_kv + e, b],
            part_recv.at[slot, b],
            near * per_kv + e,
        )

    def cross_copy(b):
        return remote(
            crossing.at[b],
            arrived.at[me, b],
            part_send.at[mirror, b],
            part_recv.at[me, b],
            mirror,
        )

    def part_wait(slot, b):
        remote(
            crossing.at[b],
            arrived.at[slot, b],
            part_send.at[slot, b],
            part_recv.at[slot, b],
            mirror,
        ).wait_recv()

    part_rows = pl.ds(pl.multiple_of(lax.rem(me, per_kv) * rows, rows), rows)

    def add_own(g):
        def own(b, c):
            row_sum[b] = jnp.zeros(row_sum.shape[1:], f32)

            @pl.when(used(me, b))
            def _():
                row_sum[b] = stage[g, b, :, part_rows, :].astype(f32)

            return c

        lax.fori_loop(0, blocks, own, 0)

    def add_peers(shift):
        def peer(step, carry):
            source = near * per_kv + lax.rem(me + step, per_kv)
            slot = lax.rem(source + shift, n)

            def one(b, c):
                @pl.when(used(source, b))
                def _():
                    part_wait(slot, b)
                    row_sum[b] += arrived[slot, b].astype(f32)

                return c

            lax.fori_loop(0, blocks, one, 0)
            return carry

        lax.fori_loop(1, per_kv, peer, 0)

    def cross():
        add_own(1 - near)
        add_peers(n // 2)

        def pack(b, c):
            crossing[b] = row_sum[b].astype(bf16)
            return c

        lax.fori_loop(0, blocks, pack, 0)

        def go(b, c):
            @pl.when(used_near(near, b))
            def _():
                cross_copy(b).start()

            return c

        lax.fori_loop(0, blocks, go, 0)

    def wanted(a, j):
        top = jnp.where(a == 0, mine[0], mine[1])
        if j == slots - 1:
            return jnp.int32(0) * top
        return jnp.maximum(top - j, 0)

    def attend(g, a):
        columns = pl.ds(pl.multiple_of(g * head_dim, head_dim), head_dim)
        v_columns = pl.ds(pl.multiple_of((kv_heads + g) * head_dim, head_dim), head_dim)
        for j in range(slots):
            here = pl.ds(j * block_len, block_len)
            position = wanted(a, j)
            k_block = kv_at[position, :, columns]
            kcat[here, :] = k_block
            vcat[here, :] = kv_at[position, :, v_columns]
            kcat_t[:, here] = k_block.T
            if j == 0:
                key_at = lax.broadcasted_iota(jnp.int32, (block_len, wide), 0)
                query_at = lax.broadcasted_iota(jnp.int32, (block_len, wide), 1) % block_len
                bias[here, :] = jnp.where(key_at <= query_at, 0.0, -jnp.inf)
            else:
                top = jnp.where(a == 0, mine[0], mine[1])
                if j == slots - 1:
                    target, real = jnp.int32(0), top > window
                else:
                    target, real = top - j, top >= j
                hits = [jnp.where(listed_ref[a, e] == target, 1, 0) for e in range(slots)]
                hit = jnp.where(real, functools.reduce(jnp.maximum, hits), 0)
                off = jnp.where(hit > 0, 0.0, -jnp.inf)
                bias[here, :] = jnp.full((block_len, wide), off, f32)
        dk_acc[...] = jnp.zeros_like(dk_acc)
        dv_acc[...] = jnp.zeros_like(dv_acc)
        query_rows = pl.ds(pl.multiple_of(a * block_len, block_len), block_len)

        def pair(i, carry):
            @pl.when(i > 0)
            def _():
                dq_start(g, a, i - 1)

            first = g * group_size + 2 * i

            def two(ref):
                return ref[pl.ds(first, 2), query_rows, :].reshape(wide, head_dim)

            q2 = two(q_heads)
            do2 = two(do_heads)
            scores = dot(kcat[...], q2, NT) * scale + bias[...]
            grad_probs = dot(vcat[...], do2, NT)
            row_max = jnp.max(scores, axis=0, keepdims=True)
            weights = jnp.exp(scores - row_max)
            probs = weights * (1.0 / jnp.sum(weights, axis=0, keepdims=True))
            low = probs.astype(bf16)
            delta = jnp.sum(low.astype(f32) * grad_probs, axis=0, keepdims=True)
            grad_scores = (probs * (grad_probs - delta)).astype(bf16)
            dq = (dot(kcat_t[...], grad_scores, NN) * scale).astype(bf16)
            for e in range(2):
                at = pl.ds(pl.multiple_of((first + e) * head_dim, head_dim), head_dim)
                dq_stage[a, at, :] = dq[:, e * block_len : (e + 1) * block_len]
            dk_acc[...] += dot(grad_scores, q2, NN)
            dv_acc[...] += dot(low, do2, NN)
            return carry

        lax.fori_loop(0, pairs, pair, 0)
        for j in range(slots):
            here = pl.ds(j * block_len, block_len)
            position = wanted(a, j)
            total[position, 0] += (dk_acc[here, :] * scale).T
            total[position, 1] += dv_acc[here, :].T
        dq_start(g, a, pairs - 1)

    def step_of(step, carry):
        phase, a = step // 2, lax.rem(step, 2)
        g = jnp.where(phase == 0, 1 - near, near)

        def arrivals(position, c):
            low_part = (
                (position <= me) & (position >= me - window) | (position == 0)
            )
            due = jnp.where(a == 0, low_part, used(me, position) & jnp.logical_not(low_part))
            other = (position != mine[0]) & (position != mine[1])
            other = other & (position != owned[0]) & (position != owned[1])

            @pl.when(due & other & (phase == 0))
            def _():
                kv_wait(position)

            return c

        lax.fori_loop(0, blocks, arrivals, 0)

        @pl.when(a == 0)
        def _():
            total[...] = jnp.zeros_like(total)

        @pl.when(step == 2 * kv_heads - 1)
        def _():
            cross()

        attend(g, a)

        @pl.when(a == 1)
        def _():
            def finish(b, c):
                @pl.when(used(me, b))
                def _():
                    stage[g, b] = total[b].astype(bf16)

                return c

            lax.fori_loop(0, blocks, finish, 0)

            def send(b, c):
                for e in range(per_kv):
                    @pl.when(used(me, b) & (lax.rem(me, per_kv) != e))
                    def _():
                        part_copy(g, e, b).start()

                return c

            lax.fori_loop(0, blocks, send, 0)

        return carry

    lax.fori_loop(0, 2 * kv_heads, step_of, 0)

    own_rows = pl.ds(pl.multiple_of(me * wide, wide), wide)
    for a in range(2):
        at = pl.ds(pl.multiple_of(me * wide + a * block_len, block_len), block_len)
        dq_out[:, at] = dq_stage[a, own_rows, :]

    add_own(near)
    add_peers(0)

    def crossed(b, c):
        @pl.when(used_near(1 - near, b))
        def _():
            part_wait(mirror, b)
            row_sum[b] += arrived[mirror, b].astype(f32)

        return c

    lax.fori_loop(0, blocks, crossed, 0)
    for b in range(blocks):
        at = 2 * b if b < n else 2 * (blocks - 1 - b) + 1
        here = pl.ds(at * block_len, block_len)
        dk_out[:, here] = row_sum[b, 0].astype(bf16)
        dv_out[:, here] = row_sum[b, 1].astype(bf16)

    def finish_dq(step, carry):
        other = lax.rem(me + step, n)
        for a in range(2):
            remote(
                dq_stage.at[a, pl.ds(0, wide), :],
                dq_out.at[:, pl.ds(pl.multiple_of(other * wide + a * block_len, block_len), block_len)],
                dq_send.at[a, other],
                dq_recv.at[a, other],
                other,
            ).wait_recv()
            dq_copy(0, a, other)[1].wait_send()
        return carry

    lax.fori_loop(1, n, finish_dq, 0)

    for half in range(2):

        @pl.when(used_near(1 - near, mine[half]))
        def _():
            kv_copy(half, mirror).wait_send()

        for step in range(1, per_kv):

            @pl.when(used(peer_of(step), mine[half]))
            def _():
                kv_copy(half, peer_of(step)).wait_send()

            @pl.when(used_near(near, owned[half]) & used(peer_of(step), owned[half]))
            def _():
                kv_forward(half, peer_of(step)).wait_send()

    def sent(b, c):
        for e in range(per_kv):
            for g in range(kv_heads):

                @pl.when(used(me, b) & (lax.rem(me, per_kv) != e))
                def _():
                    part_copy(g, e, b).wait_send()

        @pl.when(used_near(near, b))
        def _():
            cross_copy(b).wait_send()

        return c

    lax.fori_loop(0, blocks, sent, 0)


def fused(queries, grad_out, kv, listed, sizes):
    n, block_len, head_dim, kv_heads, group_size, slots = sizes
    blocks = 2 * n
    keys = slots * block_len
    tokens = 2 * block_len
    rows = kv_heads * head_dim // n
    f32, bf16 = jnp.float32, jnp.bfloat16
    dma = pltpu.SemaphoreType.DMA
    vmem = pl.BlockSpec(memory_space=pltpu.VMEM)
    return pl.pallas_call(
        functools.partial(fused_kernel, sizes),
        in_specs=[pl.BlockSpec(memory_space=pltpu.SMEM), vmem, vmem, vmem],
        out_specs=[vmem] * 3,
        out_shape=[
            jax.ShapeDtypeStruct((kv_heads * group_size * head_dim // n, n * tokens), bf16),
            jax.ShapeDtypeStruct((rows, n * tokens), bf16),
            jax.ShapeDtypeStruct((rows, n * tokens), bf16),
        ],
        scratch_shapes=[
            pltpu.VMEM((kv_heads * group_size, tokens, head_dim), bf16),
            pltpu.VMEM((kv_heads * group_size, tokens, head_dim), bf16),
            pltpu.VMEM((blocks, block_len, 2 * kv_heads * head_dim), bf16),
            pltpu.VMEM((keys, head_dim), bf16),
            pltpu.VMEM((keys, head_dim), bf16),
            pltpu.VMEM((head_dim, keys), bf16),
            pltpu.VMEM((keys, 2 * block_len), f32),
            pltpu.VMEM((keys, head_dim), f32),
            pltpu.VMEM((keys, head_dim), f32),
            pltpu.VMEM((blocks, 2, head_dim, block_len), f32),
            pltpu.VMEM((2, kv_heads * group_size * head_dim, block_len), bf16),
            pltpu.VMEM((kv_heads, blocks, 2, head_dim, block_len), bf16),
            pltpu.VMEM((n, blocks, 2, rows, block_len), bf16),
            pltpu.VMEM((blocks, 2, rows, block_len), f32),
            pltpu.VMEM((blocks, 2, rows, block_len), bf16),
            dma((2, n)),
            dma((blocks,)),
            dma((2, n)),
            dma((2, n)),
            dma((n, blocks)),
            dma((n, blocks)),
        ],
        compiler_params=pltpu.CompilerParams(collective_id=0, has_side_effects=True),
        name="attention_backward_exchange",
    )(listed, queries, grad_out, kv)


def per_device(queries, key_vectors, values, grad_out, key_blocks):
    n = lax.axis_size("seq")
    me = lax.axis_index("seq")
    tokens, q_heads, head_dim = queries.shape
    block_len = tokens // 2
    kv_heads = key_vectors.shape[1]
    group_size = q_heads // kv_heads
    slots = key_blocks.shape[1]
    window = slots - 2
    blocks = 2 * n

    kv = jnp.concatenate(
        [key_vectors.reshape(tokens, -1), values.reshape(tokens, -1)], axis=1
    )
    positions = jnp.stack([me, blocks - 1 - me])
    back = jnp.concatenate(
        [jnp.zeros((1,), jnp.int32), jnp.arange(1, window + 1, dtype=jnp.int32)]
    )
    near = positions[:, None] - back[None, :]
    near_hit = jnp.any(key_blocks[:, None, :] == near[:, :, None], axis=2) & (near >= 0)
    sink_hit = jnp.any(key_blocks == 0, axis=1) & (positions > window)
    listed = jnp.concatenate([near_hit, sink_hit[:, None]], axis=1).astype(jnp.int32)
    wanted = jnp.concatenate(
        [jnp.maximum(near, 0), jnp.zeros((2, 1), jnp.int32)], axis=1
    )
    stored = jnp.where(wanted < n, 2 * wanted, 2 * (blocks - 1 - wanted) + 1).astype(jnp.int32)

    dense = blocks <= 2 * slots
    count = blocks if dense else 2 * slots
    places = stored if dense else jnp.arange(count, dtype=jnp.int32).reshape(2, slots)
    if dense and kv_heads == 2 and q_heads == 2 * n and n % 2 == 0:
        sizes = (n, block_len, head_dim, kv_heads, group_size, slots)
        return tuple(
            fused(queries, grad_out, kv, key_blocks, sizes)
        )
    kv_all = lax.all_gather(kv, "seq", axis=0, tiled=True)
    keys = slots * block_len
    width = group_size * head_dim
    shape = (block_len, head_dim, group_size, slots)
    f32, bf16 = jnp.float32, jnp.bfloat16
    dq, dkv = pl.pallas_call(
        functools.partial(attention_kernel, shape),
        grid_spec=pltpu.PrefetchScalarGridSpec(
            num_scalar_prefetch=3,
            grid=(kv_heads, 2),
            in_specs=[
                pl.BlockSpec((block_len, width), lambda g, a, *_: (a, g)),
                pl.BlockSpec((block_len, width), lambda g, a, *_: (a, g)),
                pl.BlockSpec((n * tokens, head_dim), lambda g, a, *_: (0, g)),
                pl.BlockSpec((n * tokens, head_dim), lambda g, a, *_: (0, kv_heads + g)),
            ],
            out_specs=[
                pl.BlockSpec((width, block_len), lambda g, a, *_: (g, a)),
                pl.BlockSpec((2, head_dim, count * block_len), lambda g, a, *_: (0, g, 0)),
            ],
            scratch_shapes=[
                pltpu.VMEM((keys, head_dim), bf16),
                pltpu.VMEM((keys, head_dim), bf16),
                pltpu.VMEM((head_dim, keys), bf16),
                pltpu.VMEM((keys, 2 * block_len), f32),
                pltpu.VMEM((keys, head_dim), f32),
                pltpu.VMEM((keys, head_dim), f32),
                pltpu.VMEM((2, count, head_dim, block_len), f32),
            ],
        ),
        out_shape=[
            jax.ShapeDtypeStruct((q_heads * head_dim, tokens), bf16),
            jax.ShapeDtypeStruct((2, kv_heads * head_dim, count * block_len), bf16),
        ],
        name="attention_backward",
    )(
        stored,
        places,
        listed,
        queries.reshape(tokens, -1),
        grad_out.reshape(tokens, -1),
        kv_all,
        kv_all,
    )
    dq_rows = lax.all_to_all(dq, "seq", split_axis=0, concat_axis=1, tiled=True)
    rows = kv_heads * head_dim // n
    parts = lax.all_to_all(
        dkv.reshape(2, n, rows, count * block_len), "seq", split_axis=1, concat_axis=1, tiled=True
    )
    if dense:
        dkv_rows = jnp.sum(parts.astype(f32), axis=1).astype(bf16)
    else:
        dkv_rows = placed(parts.reshape(2, n, rows, 2, slots, block_len)).astype(bf16)
    return (dq_rows, dkv_rows[0], dkv_rows[1])


def placed(parts):
    kinds, n, rows, _, slots, block_len = parts.shape
    by_position = jnp.concatenate([parts[:, :, :, 0], parts[:, ::-1, :, 1]], axis=1)
    by_position = by_position.astype(jnp.float32)
    total = by_position[:, :, :, 0]
    for back in range(1, slots - 1):
        total = total.at[:, : 2 * n - back].add(by_position[:, back:, :, back])
    total = total.at[:, 0].add(jnp.sum(by_position[:, :, :, slots - 1], axis=1))
    stored = jnp.stack([total[:, :n], total[:, n:][:, ::-1]], axis=2)
    stored = stored.reshape(kinds, 2 * n, rows, block_len)
    return jnp.transpose(stored, (0, 2, 1, 3)).reshape(kinds, rows, 2 * n * block_len)


def solution(mesh):
    return jax.shard_map(
        per_device,
        mesh=mesh,
        in_specs=(
            P("seq", "head", None),
            P("seq", "head", None),
            P("seq", "head", None),
            P("seq", "head", None),
            P("seq", None),
        ),
        out_specs=(P(("head", "seq"), None), P(("head", "seq"), None), P(("head", "seq"), None)),
        check_vma=False,
    )
```
